256 devices in a mesh: ta: 4 (over y), gz: 8 (over x, core), gy: 8 (over z).
Axes of the slice: x: 4, y: 4, z: 8, core: 2. Of those that a mesh axis runs over, the one named last changes fastest.
Arguments:
- source: float32 [2, 3, 8, 32, 1024], P(None, None, 'ta', 'gz', 'gy'), may hold values from -40 to 40
- fat_links: bfloat16 [2, 4, 2, 3, 3, 8, 32, 1024], P(None, None, None, None, None, 'ta', 'gz', 'gy'), may hold values from -1.25 to 1.25
- long_links: bfloat16 [2, 4, 2, 3, 3, 8, 32, 1024], P(None, None, None, None, None, 'ta', 'gz', 'gy'), may hold values from -0.625 to 0.625
Outputs:
- solution: float32 [2, 3, 8, 32, 1024], P(None, None, 'ta', 'gz', 'gy')
- true_residual: float32 [2, 3, 8, 32, 1024], P(None, None, 'ta', 'gz', 'gy')
The draws below stay inside these ranges and needn't reach their ends.
All inputs are finite; a program needn't handle non-finite values.
Results may differ from the reference program's by a relative error of at most 0.00085.
Values may be sent and summed in bfloat16 or wider, within the bound.
A program may use at most 128 MiB of HBM per device.

```python
import jax
import jax.numpy as jnp

NX = 32
ITERS = 8
NTH = 8
NZ = 32
NYX = 1024


def draw_source(key, part):
    base = jax.random.normal(key, (2, 3, NTH, NZ, NYX), jnp.float32)
    base = jnp.clip(base, -3.5, 3.5)
    rows = jnp.arange(NTH, dtype=jnp.float32) / max(NTH - 1, 1)
    scale = 3.0 ** rows
    value = base * scale[None, None, :, None, None]
    return jnp.clip(value, -40.0, 40.0)


def steps_of(own_key, shape, cuts, least, top_value):
    def one(dim, parts):
        draws = jax.random.uniform(jax.random.fold_in(jax.random.fold_in(own_key, 6), dim), (parts,), jnp.float32, least / len(cuts), top_value / len(cuts))
        return jnp.repeat(jnp.exp(draws), shape[dim] // parts).reshape((-1,) + (1,) * (len(shape) - dim - 1))

    loudness = one(*cuts[0])
    for cut in cuts[1:]:
        loudness = loudness * one(*cut)
    return loudness


def gaussian(rng, dims, spread, bound, pieces=(), kind=jnp.bfloat16):
    entries = spread * jax.random.normal(rng, dims, jnp.float32)
    if pieces:
        entries = entries * steps_of(rng, dims, pieces, -0.22, 0.18)
    return jnp.clip(entries, -bound, bound).astype(kind)


def setup_inputs(seed: int = 0) -> dict:
    seeds = jax.random.split(jax.random.key(seed), 4)
    source = draw_source(jax.random.fold_in(seeds[3], 71), 0)
    fat_links = gaussian(seeds[1], (2, 4, 2, 3, 3, NTH, NZ, NYX), 0.2, 1.25, ((5, 4), (6, 8), (7, 8)))
    long_links = gaussian(seeds[2], (2, 4, 2, 3, 3, NTH, NZ, NYX), 0.1, 0.625, ((5, 4), (6, 8), (7, 8)))
    return dict(source=source, fat_links=fat_links, long_links=long_links)


mass_squared = 0.1


def mat_vec(link, vector):
    real_a, imag_a = link[0], link[1]
    real_v, imag_v = vector[0], vector[1]
    real_o = jnp.sum(real_a * real_v[None] - imag_a * imag_v[None], axis=1)
    imag_o = jnp.sum(real_a * imag_v[None] + imag_a * real_v[None], axis=1)
    return jnp.stack([real_o, imag_o])


def adj_vec(link, vector):
    real_a, imag_a = link[0], link[1]
    real_v, imag_v = vector[0], vector[1]
    real_o = jnp.sum(real_a * real_v[:, None] + imag_a * imag_v[:, None], axis=0)
    imag_o = jnp.sum(real_a * imag_v[:, None] - imag_a * real_v[:, None], axis=0)
    return jnp.stack([real_o, imag_o])


def parity_mask(z_len, yx_len):
    zeds = jnp.arange(z_len, dtype=jnp.int32)[:, None]
    cells = jnp.arange(yx_len, dtype=jnp.int32)[None, :]
    return ((zeds + cells // NX + cells % NX) % 2) == 1


def roll_x(field, shift):
    shape = field.shape
    folded = field.reshape(shape[:-1] + (shape[-1] // NX, NX))
    return jnp.roll(folded, shift, axis=-1).reshape(shape)


def reference(source, fat_links, long_links):
    mask = parity_mask(source.shape[3], source.shape[4])

    def dslash(src, dst, srcp):
        select = mask if dst == 0 else jnp.logical_not(mask)
        total = jnp.zeros(src.shape, jnp.float32)
        for mu in range(4):
            fat_dst = fat_links[dst, mu].astype(jnp.float32)
            long_dst = long_links[dst, mu].astype(jnp.float32)
            back1 = adj_vec(fat_links[srcp, mu].astype(jnp.float32), src)
            back3 = adj_vec(long_links[srcp, mu].astype(jnp.float32), src)
            if mu == 0:
                one = jnp.where(select, jnp.roll(src, -1, 2), src)
                three = jnp.where(select, jnp.roll(src, -2, 2), jnp.roll(src, -1, 2))
                low1 = jnp.where(select, back1, jnp.roll(back1, 1, 2))
                low3 = jnp.where(select, jnp.roll(back3, 1, 2), jnp.roll(back3, 2, 2))
            elif mu == 1:
                one = jnp.roll(src, -1, 3)
                three = jnp.roll(src, -3, 3)
                low1 = jnp.roll(back1, 1, 3)
                low3 = jnp.roll(back3, 3, 3)
            elif mu == 2:
                one = jnp.roll(src, -NX, 4)
                three = jnp.roll(src, -3 * NX, 4)
                low1 = jnp.roll(back1, NX, 4)
                low3 = jnp.roll(back3, 3 * NX, 4)
            else:
                one = roll_x(src, -1)
                three = roll_x(src, -3)
                low1 = roll_x(back1, 1)
                low3 = roll_x(back3, 3)
            total = total + (mat_vec(fat_dst, one) + mat_vec(long_dst, three) - low1 - low3)
        return total

    def normal_op(vector):
        return mass_squared * vector - dslash(dslash(vector, 1, 0), 0, 1)

    solution = jnp.zeros(source.shape, jnp.float32)
    residual = source
    direction = source
    norm_now = jnp.sum(residual * residual)
    for step in range(ITERS):
        image = normal_op(direction)
        alpha = norm_now / jnp.sum(direction * image)
        solution = solution + alpha * direction
        residual = residual - alpha * image
        norm_next = jnp.sum(residual * residual)
        direction = residual + (norm_next / norm_now) * direction
        norm_now = norm_next
    return solution, source - normal_op(solution)
```

```python
import functools

import jax
import jax.numpy as jnp
from jax import lax
from jax.experimental import pallas as pl
from jax.experimental.pallas import tpu as pltpu
from jax.sharding import PartitionSpec as P

NX = 32
BLOCKS = 4
MASS = 0.1
AXES = ("ta", "gz", "gy")
SIZES = {"ta": 4, "gz": 8, "gy": 8}
STAGES = ("gz", "ta", "gy")
DOTS = 9
TILE = (8, 128)


def iota(axis):
    return lax.broadcasted_iota(jnp.int32, TILE, axis)


class Grid:
    def __init__(self):
        sub, lane = iota(0), iota(1)
        self.row, self.z = sub // 4, sub % 4
        self.lane, self.x = lane, lane % NX
        self.odd = (self.z + lane // NX + self.x) % 2 == 1


def roll(field, shift, axis):
    return pltpu.roll(field, shift % TILE[axis], axis + 1)


def z_next(g, field):
    return jnp.where(g.z < 3, roll(field, -1, 0), roll(field, 3, 0))


def z_last(g, field):
    return jnp.where(g.z > 0, roll(field, 1, 0), roll(field, -3, 0))


def from_ahead(g, axis, hops, src, ahead, select):
    if axis == "ta":
        rolled = roll(jnp.where(g.row == 0, ahead, src), 4, 0)
        return jnp.where(select, rolled, src) if hops == 1 else jnp.where(select, ahead, rolled)
    if axis == "gz":
        if hops == 1:
            return z_next(g, jnp.where(g.z == 0, ahead, src))
        return z_last(g, jnp.where(g.z < 3, ahead, src))
    if axis == "gy":
        return roll(jnp.where(g.lane < hops * NX, ahead, src), -hops * NX, 1)
    return jnp.where(g.x < NX - hops, roll(src, -hops, 1), roll(src, NX - hops, 1))


def from_behind(g, axis, hops, src, behind, select):
    if axis == "ta":
        rolled = roll(jnp.where(g.row == 1, behind, src), 4, 0)
        return jnp.where(select, src, rolled) if hops == 1 else jnp.where(select, rolled, behind)
    if axis == "gz":
        if hops == 1:
            return z_last(g, jnp.where(g.z == 3, behind, src))
        return z_next(g, jnp.where(g.z > 0, behind, src))
    if axis == "gy":
        return roll(jnp.where(g.lane >= 128 - hops * NX, behind, src), hops * NX, 1)
    return jnp.where(g.x >= hops, roll(src, hops, 1), roll(src, hops - NX, 1))


def kernel(
    b_ref,
    fat_ref,
    long_ref,
    x_out,
    t_out,
    vec,
    prev,
    xs,
    odd_f,
    own,
    back,
    halo,
    rims,
    row,
    sums1,
    sums2,
    sums3,
    kept,
    halo_send,
    halo_recv,
    rim_send,
    rim_recv,
    sum_send,
    recv1,
    recv2,
    recv3,
):
    g = Grid()
    me = {a: lax.axis_index(a) for a in AXES}

    def at(axis, by):
        return {axis: lax.rem(me[axis] + (by % SIZES[axis]), SIZES[axis])}

    mesh_id = pl.DeviceIdType.MESH
    barrier = pltpu.get_barrier_semaphore()
    for axis in AXES:
        for by in range(1, SIZES[axis]):
            pl.semaphore_signal(barrier, inc=1, device_id=at(axis, by), device_id_type=mesh_id)
    pl.semaphore_wait(barrier, sum(SIZES[a] - 1 for a in AXES))

    def halo_copies(src, slot):
        copies = []
        for n, axis in enumerate(AXES):
            for side, by in enumerate((-1, 1)):
                copies.append(
                    pltpu.make_async_remote_copy(
                        src_ref=src,
                        dst_ref=halo.at[slot, n, side],
                        send_sem=halo_send.at[slot, n, side],
                        recv_sem=halo_recv.at[slot, n, side],
                        device_id=at(axis, by),
                        device_id_type=mesh_id,
                    )
                )
        return copies

    def rim_copies(p):
        copies = []
        for n, axis in enumerate(AXES):
            for kind, links in enumerate((fat_ref, long_ref)):
                copies.append(
                    pltpu.make_async_remote_copy(
                        src_ref=links.at[p, n],
                        dst_ref=rims.at[p, n, kind],
                        send_sem=rim_send.at[p, n, kind],
                        recv_sem=rim_recv.at[p, n, kind],
                        device_id=at(axis, 1),
                        device_id_type=mesh_id,
                    )
                )
        return copies

    def selected(dst):
        return g.odd if dst == 0 else jnp.logical_not(g.odd)

    rim = [rim_copies(0), rim_copies(1)]
    for copies in rim:
        for c in copies:
            c.start()
    for p in (1, 0):
        for mu in range(4):
            for kind, links in enumerate((fat_ref, long_ref)):
                own[p, 2 * mu + kind] = links[p, mu].astype(jnp.float32)
    for p in (0, 1):
        dst = 1 - p
        for mu in range(4):
            for kind in range(2):
                hops = 1 + 2 * kind
                axis = AXES[mu] if mu < 3 else "x"
                mine = own[p, 2 * mu + kind]
                if mu < 3:
                    rim[p][2 * mu + kind].wait_recv()
                    theirs = rims[p, mu, kind].astype(jnp.float32)
                else:
                    theirs = None
                back[dst, 2 * mu + kind] = from_behind(g, axis, hops, mine, theirs, selected(dst))
    for copies in rim:
        for c in copies:
            c.wait_send()

    def ahead_terms(acc, dst, k, v):
        re, im = acc
        vr, vi = v[:3], v[3:]
        for j in range(3):
            mr, mi = own[dst, k, pl.ds(j, 3, stride=3)], own[dst, k, pl.ds(9 + j, 3, stride=3)]
            re = re + mr * vr[j][None] - mi * vi[j][None]
            im = im + mr * vi[j][None] + mi * vr[j][None]
        return re, im

    def behind_terms(acc, dst, k, v):
        re, im = acc
        vr, vi = v[:3], v[3:]
        for i in range(3):
            mr, mi = back[dst, k, pl.ds(3 * i, 3)], back[dst, k, pl.ds(9 + 3 * i, 3)]
            re = re - mr * vr[i][None] - mi * vi[i][None]
            im = im - mr * vi[i][None] + mi * vr[i][None]
        return re, im

    def half(src_ref, dst):
        slot = dst
        copies = halo_copies(src_ref, slot)
        for c in copies:
            c.start()
        select = selected(dst)
        src = src_ref[...]
        zero = jnp.zeros((3, *TILE), jnp.float32)
        acc = (zero, zero)
        for axis, mu in (("x", 3), ("gz", 1), ("gy", 2), ("ta", 0)):
            ahead = behind = None
            if mu < 3:
                copies[2 * mu].wait_recv()
                copies[2 * mu + 1].wait_recv()
                ahead, behind = halo[slot, mu, 0], halo[slot, mu, 1]
            for kind in range(2):
                k, hops = 2 * mu + kind, 1 + 2 * kind
                acc = ahead_terms(acc, dst, k, from_ahead(g, axis, hops, src, ahead, select))
                acc = behind_terms(acc, dst, k, from_behind(g, axis, hops, src, behind, select))
        for c in copies:
            c.wait_send()
        return jnp.concatenate(acc, axis=0)

    def first_half(src):
        odd_f[...] = half(src, 1)

    def second_half(src):
        return MASS * src[...] - half(odd_f, 0)

    def stage_copies(blk, stage):
        axis = STAGES[stage]
        sums, recv = (sums1, sums2, sums3)[stage], (recv1, recv2, recv3)[stage]
        size = SIZES[axis]
        out, into = [], []
        for by in range(1, size):
            there = lax.rem(me[axis] + by, size)
            out.append(
                pltpu.make_async_remote_copy(
                    src_ref=row,
                    dst_ref=sums.at[blk, me[axis]],
                    send_sem=sum_send.at[by - 1],
                    recv_sem=recv.at[blk, me[axis]],
                    device_id={axis: there},
                    device_id_type=mesh_id,
                )
            )
            into.append(
                pltpu.make_async_remote_copy(
                    src_ref=row,
                    dst_ref=sums.at[blk, there],
                    send_sem=sum_send.at[by - 1],
                    recv_sem=recv.at[blk, there],
                    device_id={axis: there},
                    device_id_type=mesh_id,
                )
            )
        return out, into

    def stage_start(blk, stage, line):
        row[...] = line
        sums = (sums1, sums2, sums3)[stage]
        sums[blk, me[STAGES[stage]]] = line
        for c in stage_copies(blk, stage)[0]:
            c.start()

    def stage_end(blk, stage):
        out, into = stage_copies(blk, stage)
        for c in out:
            c.wait_send()
        for c in into:
            c.wait_recv()
        return jnp.sum((sums1, sums2, sums3)[stage][blk], axis=0)

    lane = lax.broadcasted_iota(jnp.int32, (1, 128), 1)

    def local_dots():
        r, w, q = vec[0], vec[1], vec[2]
        m, v = prev[0], prev[1]
        pairs = ((r, r), (r, w), (w, w), (w, q), (r, m), (w, m), (w, v), (m, m), (m, v))
        line = jnp.zeros((1, 128), jnp.float32)
        for n, (a, b) in enumerate(pairs):
            line = line + jnp.where(lane == n, jnp.sum(jnp.sum(a * b, axis=0)), 0.0)
        return line

    def coefficients(line):
        rr, rw, ww, wq, rm, wm, wv, mm, mv = (
            jnp.broadcast_to(jnp.sum(jnp.where(lane == n, line, 0.0)), TILE) for n in range(DOTS)
        )
        step = rr / rw
        u = 1.0 / (1.0 - step * rr * kept[...])
        f, h = -u * step, 1.0 - u
        rr1 = u * u * rr + f * f * ww + h * h * mm + 2.0 * (u * f * rw + u * h * rm + f * h * wm)
        rw1 = u * u * rw + f * f * wq + h * h * mv + 2.0 * (u * f * ww + u * h * wm + f * h * wv)
        step1 = rr1 / rw1
        u1 = 1.0 / (1.0 - step1 * rr1 / (step * rr * u))
        kept[...] = 1.0 / (step1 * rr1 * u1)
        return step, u, step1, u1

    def update(line, last):
        step, u, step1, u1 = coefficients(line)
        h, h1 = 1.0 - u, 1.0 - u1
        first = [
            u * (vec[k] - step * vec[k + 1]) + h * prev[k] for k in range(1 if last else 4)
        ]
        x, x0 = xs[0], xs[1]
        x1 = u * (x + step * vec[0]) + h * x0
        xs[1] = x1
        xs[0] = u1 * (x1 + step1 * first[0]) + h1 * x
        if not last:
            second = [u1 * (first[k] - step1 * first[k + 1]) + h1 * vec[k] for k in range(3)]
            for k in range(3):
                vec[k] = second[k]
            for k in range(4):
                prev[k] = first[k]

    vec[0] = b_ref[...]
    prev[...] = jnp.zeros_like(prev)
    xs[...] = jnp.zeros_like(xs)
    kept[...] = jnp.zeros_like(kept)

    def opening(k, carry):
        first_half(vec.at[k])
        vec[k + 1] = second_half(vec.at[k])
        return carry

    lax.fori_loop(0, 2, opening, 0)

    def block(blk, carry):
        stage_start(blk, 0, local_dots())
        first_half(vec.at[2])
        stage_start(blk, 1, stage_end(blk, 0))
        vec[3] = second_half(vec.at[2])
        stage_start(blk, 2, stage_end(blk, 1))
        first_half(vec.at[3])
        vec[4] = second_half(vec.at[3])
        update(stage_end(blk, 2), False)
        return carry

    lax.fori_loop(0, BLOCKS - 1, block, 0)
    line = local_dots()
    for stage in range(3):
        stage_start(BLOCKS - 1, stage, line)
        line = stage_end(BLOCKS - 1, stage)
    update(line, True)
    x_out[...] = xs[0]
    first_half(xs.at[0])
    t_out[...] = b_ref[...] - second_half(xs.at[0])


def per_device(source, fat_links, long_links):
    f32 = jnp.float32
    field = (6, *TILE)
    dma = pltpu.SemaphoreType.DMA
    fat = fat_links.reshape(2, 4, 18, *TILE)
    long = long_links.reshape(2, 4, 18, *TILE)
    vmem = pl.BlockSpec(memory_space=pltpu.VMEM)
    x, t = pl.pallas_call(
        kernel,
        out_shape=(jax.ShapeDtypeStruct(field, f32), jax.ShapeDtypeStruct(field, f32)),
        in_specs=[vmem] * 3,
        out_specs=(vmem, vmem),
        scratch_shapes=[
            pltpu.VMEM((5, *field), f32),
            pltpu.VMEM((4, *field), f32),
            pltpu.VMEM((2, *field), f32),
            pltpu.VMEM(field, f32),
            pltpu.VMEM((2, 8, 18, *TILE), f32),
            pltpu.VMEM((2, 8, 18, *TILE), f32),
            pltpu.VMEM((2, 3, 2, *field), f32),
            pltpu.VMEM((2, 3, 2, 18, *TILE), jnp.bfloat16),
            pltpu.VMEM((1, 128), f32),
            pltpu.VMEM((BLOCKS, SIZES[STAGES[0]], 1, 128), f32),
            pltpu.VMEM((BLOCKS, SIZES[STAGES[1]], 1, 128), f32),
            pltpu.VMEM((BLOCKS, SIZES[STAGES[2]], 1, 128), f32),
            pltpu.VMEM(TILE, f32),
            dma((2, 3, 2)),
            dma((2, 3, 2)),
            dma((2, 3, 2)),
            dma((2, 3, 2)),
            dma((7,)),
            dma((BLOCKS, SIZES[STAGES[0]])),
            dma((BLOCKS, SIZES[STAGES[1]])),
            dma((BLOCKS, SIZES[STAGES[2]])),
        ],
        compiler_params=pltpu.CompilerParams(
            collective_id=0, has_side_effects=True, vmem_limit_bytes=32 * 1024 * 1024
        ),
    )(source.reshape(field), fat, long)
    return x.reshape(source.shape), t.reshape(source.shape)


def solution(mesh):
    field = P(None, None, "ta", "gz", "gy")
    links = P(None, None, None, None, None, "ta", "gz", "gy")
    return jax.shard_map(
        per_device,
        mesh=mesh,
        in_specs=(field, links, links),
        out_specs=(field, field),
        check_vma=False,
    )
```

```python
import jax
import jax.numpy as jnp
from jax import lax
from jax.experimental import pallas as pl
from jax.experimental.pallas import tpu as pltpu
from jax.sharding import PartitionSpec as P

NX = 32
BLOCKS = 4
MASS = 0.1
AXES = ("ta", "gz", "gy")
SIZES = {"ta": 4, "gz": 8, "gy": 8}
MEMBERS = 16
DOTS = 9
TILE = (8, 128)


def iota(axis):
    return lax.broadcasted_iota(jnp.int32, TILE, axis)


class Grid:
    def __init__(self):
        sub, lane = iota(0), iota(1)
        self.row, self.z = sub // 4, sub % 4
        self.lane, self.x = lane, lane % NX
        self.odd = (self.z + lane // NX + self.x) % 2 == 1


def roll(field, shift, axis):
    return pltpu.roll(field, shift % TILE[axis], axis + 1)


def z_next(g, field):
    return jnp.where(g.z < 3, roll(field, -1, 0), roll(field, 3, 0))


def z_last(g, field):
    return jnp.where(g.z > 0, roll(field, 1, 0), roll(field, -3, 0))


def from_ahead(g, axis, hops, src, ahead, select):
    if axis == "ta":
        rolled = roll(jnp.where(g.row == 0, ahead, src), 4, 0)
        return jnp.where(select, rolled, src) if hops == 1 else jnp.where(select, ahead, rolled)
    if axis == "gz":
        if hops == 1:
            return z_next(g, jnp.where(g.z == 0, ahead, src))
        return z_last(g, jnp.where(g.z < 3, ahead, src))
    if axis == "gy":
        return roll(jnp.where(g.lane < hops * NX, ahead, src), -hops * NX, 1)
    return jnp.where(g.x < NX - hops, roll(src, -hops, 1), roll(src, NX - hops, 1))


def from_behind(g, axis, hops, src, behind, select):
    if axis == "ta":
        rolled = roll(jnp.where(g.row == 1, behind, src), 4, 0)
        return jnp.where(select, src, rolled) if hops == 1 else jnp.where(select, rolled, behind)
    if axis == "gz":
        if hops == 1:
            return z_last(g, jnp.where(g.z == 3, behind, src))
        return z_next(g, jnp.where(g.z > 0, behind, src))
    if axis == "gy":
        return roll(jnp.where(g.lane >= 128 - hops * NX, behind, src), hops * NX, 1)
    return jnp.where(g.x >= hops, roll(src, hops, 1), roll(src, hops - NX, 1))


def kernel(
    b_hbm,
    fat_hbm,
    long_hbm,
    x_out,
    t_out,
    fat_ref,
    long_ref,
    src_b,
    vec,
    prev,
    xs,
    images,
    odd_f,
    own,
    back,
    halo,
    rims,
    row,
    sums,
    kept,
    shift,
    load,
    halo_send,
    halo_recv,
    rim_send,
    rim_recv,
    sum_send,
    sum_recv,
):
    g = Grid()
    me = {a: lax.axis_index(a) for a in AXES}
    mesh_id = pl.DeviceIdType.MESH

    def at(axis, by):
        return {axis: lax.rem(me[axis] + (by % SIZES[axis]), SIZES[axis])}

    low, high = lax.rem(me["ta"], 2), me["ta"] // 2
    groups = (("gz", low, me["ta"] + 1 - 2 * low), ("gy", high, 3 - me["ta"]))

    def peers(stage):
        axis, bit, partner = groups[stage]
        for by in range(SIZES[axis]):
            there = lax.rem(me[axis] + by, SIZES[axis])
            if by:
                yield {axis: there}, 2 * there + bit
            yield {axis: there, "ta": partner}, 2 * there + 1 - bit

    def my_place(stage):
        axis, bit, _ = groups[stage]
        return 2 * me[axis] + bit

    barrier = pltpu.get_barrier_semaphore()
    for axis in AXES:
        for by in (-1, 1):
            pl.semaphore_signal(barrier, inc=1, device_id=at(axis, by), device_id_type=mesh_id)
    loads = [
        pltpu.make_async_copy(a, c, load.at[n])
        for n, (a, c) in enumerate(((b_hbm, src_b), (fat_hbm, fat_ref), (long_hbm, long_ref)))
    ]
    for c in loads:
        c.start()
    pl.semaphore_wait(barrier, 2 * len(AXES))

    def halo_copies(fields, slot):
        copies = []
        for n, axis in enumerate(AXES):
            for side, by in enumerate((-1, 1)):
                for f, src in enumerate(fields):
                    copies.append(
                        pltpu.make_async_remote_copy(
                            src_ref=src,
                            dst_ref=halo.at[slot, f, n, side],
                            send_sem=halo_send.at[slot, f, n, side],
                            recv_sem=halo_recv.at[slot, f, n, side],
                            device_id=at(axis, by),
                            device_id_type=mesh_id,
                        )
                    )
        return copies

    def rim_copies(p):
        copies = []
        for n, axis in enumerate(AXES):
            for kind, links in enumerate((fat_ref, long_ref)):
                copies.append(
                    pltpu.make_async_remote_copy(
                        src_ref=links.at[p, n],
                        dst_ref=rims.at[p, n, kind],
                        send_sem=rim_send.at[p, n, kind],
                        recv_sem=rim_recv.at[p, n, kind],
                        device_id=at(axis, 1),
                        device_id_type=mesh_id,
                    )
                )
        return copies

    def selected(dst):
        return g.odd if dst == 0 else jnp.logical_not(g.odd)

    rim = [rim_copies(0), rim_copies(1)]

    def own_links(p):
        for mu in range(4):
            for kind, links in enumerate((fat_ref, long_ref)):
                own[p, 2 * mu + kind] = links[p, mu].astype(jnp.float32)

    def back_links(p):
        dst = 1 - p
        for mu in (3, 1, 2, 0):
            for kind in range(2):
                theirs = None
                if mu < 3:
                    rim[p][2 * mu + kind].wait_recv()
                    theirs = rims[p, mu, kind].astype(jnp.float32)
                axis = AXES[mu] if mu < 3 else "x"
                back[dst, 2 * mu + kind] = from_behind(
                    g, axis, 1 + 2 * kind, own[p, 2 * mu + kind], theirs, selected(dst)
                )

    def ahead_terms(acc, dst, k, v):
        re, im = acc
        vr, vi = v[:3], v[3:]
        for j in range(3):
            mr, mi = own[dst, k, pl.ds(j, 3, stride=3)], own[dst, k, pl.ds(9 + j, 3, stride=3)]
            re = re + mr * vr[j][None] - mi * vi[j][None]
            im = im + mr * vi[j][None] + mi * vr[j][None]
        return re, im

    def behind_terms(acc, dst, k, v):
        re, im = acc
        vr, vi = v[:3], v[3:]
        for i in range(3):
            mr, mi = back[dst, k, pl.ds(3 * i, 3)], back[dst, k, pl.ds(9 + 3 * i, 3)]
            re = re - mr * vr[i][None] - mi * vi[i][None]
            im = im - mr * vi[i][None] + mi * vr[i][None]
        return re, im

    def half(fields, dst, between=None):
        slot = dst
        copies = halo_copies(fields, slot)
        for c in copies:
            c.start()
        if between is not None:
            between()
        select = selected(dst)
        zero = jnp.zeros((3, *TILE), jnp.float32)
        accs = [(zero, zero) for _ in fields]
        per_axis = 2 * len(fields)
        for axis, mu in (("x", 3), ("gz", 1), ("gy", 2), ("ta", 0)):
            if mu < 3:
                for c in copies[per_axis * mu : per_axis * (mu + 1)]:
                    c.wait_recv()
            for f, field in enumerate(fields):
                src, acc = field[...], accs[f]
                ahead = behind = None
                if mu < 3:
                    ahead, behind = halo[slot, f, mu, 0], halo[slot, f, mu, 1]
                for kind in range(2):
                    k, hops = 2 * mu + kind, 1 + 2 * kind
                    acc = ahead_terms(acc, dst, k, from_ahead(g, axis, hops, src, ahead, select))
                    acc = behind_terms(acc, dst, k, from_behind(g, axis, hops, src, behind, select))
                accs[f] = acc
        for c in copies:
            c.wait_send()
        return [jnp.concatenate(acc, axis=0) for acc in accs]

    def first_half(fields, between=None):
        for f, value in enumerate(half(fields, 1, between)):
            odd_f[f] = value

    def second_half(fields, diagonal, between=None):
        odds = [odd_f.at[f] for f in range(len(fields))]
        return [diagonal * v[...] - d for v, d in zip(fields, half(odds, 0, between))]

    def stage_copies(blk, stage, place_of):
        copies = []
        for n, (device, place) in enumerate(peers(stage)):
            spot = my_place(stage) if place_of == "mine" else place
            copies.append(
                pltpu.make_async_remote_copy(
                    src_ref=row,
                    dst_ref=sums.at[stage, blk, spot],
                    send_sem=sum_send.at[n],
                    recv_sem=sum_recv.at[stage, blk, spot],
                    device_id=device,
                    device_id_type=mesh_id,
                )
            )
        return copies

    def stage_start(blk, stage, line):
        row[...] = line
        sums[stage, blk, my_place(stage)] = line
        for c in stage_copies(blk, stage, "mine"):
            c.start()

    def stage_end(blk, stage):
        for c in stage_copies(blk, stage, "theirs"):
            c.wait_send()
            c.wait_recv()
        return jnp.sum(sums[stage, blk], axis=0)

    lane = lax.broadcasted_iota(jnp.int32, (1, 128), 1)

    def local_dots():
        r, w, q = vec[0], vec[1], vec[2]
        m, v = prev[0], prev[1]
        pairs = ((r, r), (r, w), (w, w), (w, q), (r, m), (w, m), (w, v), (m, m), (m, v))
        line = jnp.zeros((1, 128), jnp.float32)
        for n, (a, b) in enumerate(pairs):
            line = line + jnp.where(lane == n, jnp.sum(jnp.sum(a * b, axis=0)), 0.0)
        return line

    def coefficients(line):
        rr, rw, ww, wq, rm, wm, wv, mm, mv = (
            jnp.broadcast_to(jnp.sum(jnp.where(lane == n, line, 0.0)), TILE) for n in range(DOTS)
        )
        c = shift[...]
        step = rr / (rw + c * rr)
        scale = 1.0 / (1.0 - step * rr * kept[...])
        u, f, h = scale * (1.0 - step * c), -scale * step, 1.0 - scale
        rr1 = u * u * rr + f * f * ww + h * h * mm + 2.0 * (u * f * rw + u * h * rm + f * h * wm)
        rw1 = u * u * rw + f * f * wq + h * h * mv + 2.0 * (u * f * ww + u * h * wm + f * h * wv)
        mean1 = (rw1 + c * rr1) / rr1
        step1 = 1.0 / mean1
        scale1 = 1.0 / (1.0 - step1 * rr1 / (step * rr * scale))
        u1, f1, h1 = scale1 * (1.0 - step1 * c), -scale1 * step1, 1.0 - scale1
        kept[...] = 1.0 / (step1 * rr1 * scale1)
        return (step, scale, u, f, h), (step1, scale1, u1, f1, h1), mean1

    def update(line):
        (step, scale, u, f, h), (step1, scale1, u1, f1, h1), mean1 = coefficients(line)
        first = [u * vec[k] + f * vec[k + 1] + h * prev[k] for k in range(4)]
        second = [u1 * first[k] + f1 * first[k + 1] + h1 * vec[k] for k in range(3)]
        x, x0 = xs[0], xs[1]
        x1 = scale * (x + step * vec[0]) + h * x0
        xs[1] = x1
        xs[0] = scale1 * (x1 + step1 * first[0]) + h1 * x
        d = mean1 - shift[...]
        shift[...] = mean1
        for stack, place in ((second, vec), (first, prev)):
            for k in range(len(stack)):
                place[k] = stack[0]
                stack = [b - d * a for a, b in zip(stack, stack[1:])]

    def last_update(line):
        (step, scale, u, f, h), (step1, scale1, u1, f1, h1), _ = coefficients(line)
        c = shift[...]
        r, w, q, m, v = vec[0], vec[1], vec[2], prev[0], prev[1]
        x, x0, ax, ax0 = xs[0], xs[1], images[0], images[1]
        r1 = u * r + f * w + h * m
        x1 = scale * (x + step * r) + h * x0
        x_out[...] = scale1 * (x1 + step1 * r1) + h1 * x
        ar = w + c * r
        ar1 = u * ar + f * (q + c * w) + h * (v + c * m)
        ax1 = scale * (ax + step * ar) + h * ax0
        t_out[...] = src_b[...] - (scale1 * (ax1 + step1 * ar1) + h1 * ax)

    loads[0].wait()
    vec[0] = src_b[...]
    prev[...] = jnp.zeros_like(prev)
    xs[...] = jnp.zeros_like(xs)
    kept[...] = jnp.zeros_like(kept)
    shift[...] = jnp.zeros_like(shift)

    def links_for_first():
        loads[1].wait()
        loads[2].wait()
        for copies in rim:
            for c in copies:
                c.start()
        own_links(0)
        own_links(1)
        back_links(0)

    def links_for_second():
        back_links(1)
        for copies in rim:
            for c in copies:
                c.wait_send()

    first_half([src_b], links_for_first)
    (vec[1],) = second_half([src_b], MASS, links_for_second)
    first_half([vec.at[1]])
    (vec[2],) = second_half([vec.at[1]], MASS)

    def block(blk, carry):
        diagonal = MASS - shift[...]
        stage_start(blk, 0, local_dots())
        first_half([vec.at[2]])
        (vec[3],) = second_half([vec.at[2]], diagonal)
        stage_start(blk, 1, stage_end(blk, 0))
        first_half([vec.at[3]])
        (vec[4],) = second_half([vec.at[3]], diagonal)
        update(stage_end(blk, 1))
        return carry

    lax.fori_loop(0, BLOCKS - 1, block, 0)
    stage_start(BLOCKS - 1, 0, local_dots())
    both = [xs.at[0], xs.at[1]]
    first_half(both)
    stage_start(BLOCKS - 1, 1, stage_end(BLOCKS - 1, 0))
    images[0], images[1] = second_half(both, MASS)
    last_update(stage_end(BLOCKS - 1, 1))


def per_device(source, fat_links, long_links):
    f32 = jnp.float32
    field = (6, *TILE)
    dma = pltpu.SemaphoreType.DMA
    fat = fat_links.reshape(2, 4, 18, *TILE)
    long = long_links.reshape(2, 4, 18, *TILE)
    vmem = pl.BlockSpec(memory_space=pltpu.VMEM)
    hbm = pl.BlockSpec(memory_space=pltpu.HBM)
    x, t = pl.pallas_call(
        kernel,
        out_shape=(jax.ShapeDtypeStruct(field, f32), jax.ShapeDtypeStruct(field, f32)),
        in_specs=[hbm] * 3,
        out_specs=(vmem, vmem),
        scratch_shapes=[
            pltpu.VMEM(fat.shape, fat.dtype),
            pltpu.VMEM(long.shape, long.dtype),
            pltpu.VMEM(field, f32),
            pltpu.VMEM((5, *field), f32),
            pltpu.VMEM((4, *field), f32),
            pltpu.VMEM((2, *field), f32),
            pltpu.VMEM((2, *field), f32),
            pltpu.VMEM((2, *field), f32),
            pltpu.VMEM((2, 8, 18, *TILE), f32),
            pltpu.VMEM((2, 8, 18, *TILE), f32),
            pltpu.VMEM((2, 2, 3, 2, *field), f32),
            pltpu.VMEM((2, 3, 2, 18, *TILE), jnp.bfloat16),
            pltpu.VMEM((1, 128), f32),
            pltpu.VMEM((2, BLOCKS, MEMBERS, 1, 128), f32),
            pltpu.VMEM(TILE, f32),
            pltpu.VMEM(TILE, f32),
            dma((3,)),
            dma((2, 2, 3, 2)),
            dma((2, 2, 3, 2)),
            dma((2, 3, 2)),
            dma((2, 3, 2)),
            dma((MEMBERS - 1,)),
            dma((2, BLOCKS, MEMBERS)),
        ],
        compiler_params=pltpu.CompilerParams(
            collective_id=0, has_side_effects=True
        ),
    )(source.reshape(field), fat, long)
    return x.reshape(source.shape), t.reshape(source.shape)


def solution(mesh):
    field = P(None, None, "ta", "gz", "gy")
    links = P(None, None, None, None, None, "ta", "gz", "gy")
    return jax.shard_map(
        per_device,
        mesh=mesh,
        in_specs=(field, links, links),
        out_specs=(field, field),
        check_vma=False,
    )
```

```python
import jax
import jax.numpy as jnp
from jax import lax
from jax.experimental import pallas as pl
from jax.experimental.pallas import tpu as pltpu
from jax.sharding import PartitionSpec as P

NX = 32
BLOCKS = 4
MASS = 0.1
AXES = ("ta", "gz", "gy")
SIZES = {"ta": 4, "gz": 8, "gy": 8}
MEMBERS = 16
DOTS = 9
TILE = (8, 128)


def iota(axis):
    return lax.broadcasted_iota(jnp.int32, TILE, axis)


class Grid:
    def __init__(self):
        sub, lane = iota(0), iota(1)
        self.row, self.z = sub // 4, sub % 4
        self.lane, self.x = lane, lane % NX
        self.odd = (self.z + lane // NX + self.x) % 2 == 1


def roll(field, shift, axis):
    return pltpu.roll(field, shift % TILE[axis], axis + 1)


def turn(g, axis, kind, field, select):
    if axis == "ta":
        rolled = roll(field, 4, 0)
        return jnp.where(select, rolled, field) if kind == 0 else jnp.where(select, field, rolled)
    if axis == "gz":
        if kind == 0:
            return jnp.where(g.z < 3, roll(field, -1, 0), roll(field, 3, 0))
        return jnp.where(g.z > 0, roll(field, 1, 0), roll(field, -3, 0))
    return roll(field, -NX if kind == 0 else NX, 1)


def across(g, axis, kind, ahead, behind, select):
    if axis == "ta":
        rolled = roll(jnp.where(g.row == 0, ahead, behind), 4, 0)
        return jnp.where(select, rolled, behind) if kind == 0 else jnp.where(select, ahead, rolled)
    if axis == "gz":
        mixed = jnp.where(g.z == 0 if kind == 0 else g.z < 3, ahead, behind)
    else:
        mixed = jnp.where(g.lane < (NX if kind == 0 else 3 * NX), ahead, behind)
    return turn(g, axis, kind, mixed, select)


def inside(g, axis, kind, select):
    if axis == "ta":
        unselected = jnp.logical_not(select)
        first = g.row == 0
        return jnp.logical_or(unselected, first) if kind == 0 else jnp.logical_and(unselected, first)
    if axis == "gz":
        return g.z < 3 if kind == 0 else g.z == 0
    return g.lane < (3 * NX if kind == 0 else NX)


def along_x(g, by, field):
    if by > 0:
        return jnp.where(g.x < NX - by, roll(field, -by, 1), roll(field, NX - by, 1))
    return jnp.where(g.x >= -by, roll(field, -by, 1), roll(field, -by - NX, 1))


def kernel(
    b_hbm,
    fat_hbm,
    long_hbm,
    x_out,
    t_out,
    fat_ref,
    long_ref,
    src_b,
    vec,
    prev,
    xs,
    images,
    odd_f,
    mats,
    halo,
    rims,
    row,
    sums,
    kept,
    shift,
    load,
    halo_send,
    halo_recv,
    rim_send,
    rim_recv,
    sum_send,
    sum_recv,
):
    g = Grid()
    me = {a: lax.axis_index(a) for a in AXES}
    mesh_id = pl.DeviceIdType.MESH

    def at(axis, by):
        return {axis: lax.rem(me[axis] + (by % SIZES[axis]), SIZES[axis])}

    low, high = lax.rem(me["ta"], 2), me["ta"] // 2
    groups = (("gz", low, me["ta"] + 1 - 2 * low), ("gy", high, 3 - me["ta"]))

    def peers(stage):
        axis, bit, partner = groups[stage]
        for by in range(SIZES[axis]):
            there = lax.rem(me[axis] + by, SIZES[axis])
            if by:
                yield {axis: there}, 2 * there + bit
            yield {axis: there, "ta": partner}, 2 * there + 1 - bit

    def my_place(stage):
        axis, bit, _ = groups[stage]
        return 2 * me[axis] + bit

    barrier = pltpu.get_barrier_semaphore()
    for axis in AXES:
        for by in (-1, 1):
            pl.semaphore_signal(barrier, inc=1, device_id=at(axis, by), device_id_type=mesh_id)
    loads = [
        pltpu.make_async_copy(a, c, load.at[n])
        for n, (a, c) in enumerate(((b_hbm, src_b), (fat_hbm, fat_ref), (long_hbm, long_ref)))
    ]
    for c in loads:
        c.start()
    pl.semaphore_wait(barrier, 2 * len(AXES))

    def halo_copies(fields, slot):
        copies = []
        for n, axis in enumerate(AXES):
            for side, by in enumerate((-1, 1)):
                for f, src in enumerate(fields):
                    copies.append(
                        pltpu.make_async_remote_copy(
                            src_ref=src,
                            dst_ref=halo.at[slot, f, n, side],
                            send_sem=halo_send.at[slot, f, n, side],
                            recv_sem=halo_recv.at[slot, f, n, side],
                            device_id=at(axis, by),
                            device_id_type=mesh_id,
                        )
                    )
        return copies

    def rim_copies(p):
        copies = []
        for n, axis in enumerate(AXES):
            for kind, links in enumerate((fat_ref, long_ref)):
                copies.append(
                    pltpu.make_async_remote_copy(
                        src_ref=links.at[p, n],
                        dst_ref=rims.at[p, n, kind],
                        send_sem=rim_send.at[p, n, kind],
                        recv_sem=rim_recv.at[p, n, kind],
                        device_id=at(axis, 1),
                        device_id_type=mesh_id,
                    )
                )
        return copies

    def selected(dst):
        return g.odd if dst == 0 else jnp.logical_not(g.odd)

    rim = [rim_copies(0), rim_copies(1)]

    def plain(links, p, mu):
        columns = [links[p, mu, pl.ds(9 * part + j, 3, stride=3)] for part in (0, 1) for j in range(3)]
        return jnp.concatenate(columns, axis=0).astype(jnp.float32)

    def minus_adjoint(links):
        links = links.astype(jnp.float32)
        return jnp.concatenate([-links[:9], links[9:]], axis=0)

    kinds = (fat_ref, long_ref)
    X_HOPS = ((0, 1), (1, 3), (0, -1), (1, -3))

    def local_matrices(dst):
        select = selected(dst)
        for n, (kind, by) in enumerate(X_HOPS):
            if by > 0:
                mats[dst, n] = plain(kinds[kind], dst, 3)
            else:
                links = kinds[kind][1 - dst, 3].astype(jnp.float32)
                mats[dst, n] = minus_adjoint(along_x(g, by, links))
        for mu, axis in enumerate(AXES):
            for kind in range(2):
                links = kinds[1 - kind][1 - dst, mu].astype(jnp.float32)
                mats[dst, 4 + 4 * mu + kind] = jnp.where(
                    inside(g, axis, kind, select),
                    plain(kinds[kind], dst, mu),
                    minus_adjoint(turn(g, axis, kind, links, select)),
                )

    def border_matrices(dst):
        select = selected(dst)
        for mu, axis in enumerate(AXES):
            for kind in range(2):
                rim[1 - dst][2 * mu + 1 - kind].wait_recv()
                links = rims[1 - dst, mu, 1 - kind].astype(jnp.float32)
                mats[dst, 6 + 4 * mu + kind] = jnp.where(
                    inside(g, axis, kind, select),
                    minus_adjoint(turn(g, axis, kind, links, select)),
                    plain(kinds[kind], dst, mu),
                )

    def times(acc, dst, k, v):
        re, im = acc
        vr, vi = v[:3], v[3:]
        for j in range(3):
            mr, mi = mats[dst, k, pl.ds(3 * j, 3)], mats[dst, k, pl.ds(9 + 3 * j, 3)]
            re = re + mr * vr[j][None] - mi * vi[j][None]
            im = im + mr * vi[j][None] + mi * vr[j][None]
        return re, im

    def half(fields, dst, hook=None, border_hook=None):
        slot = dst
        copies = halo_copies(fields, slot)
        for c in copies:
            c.start()
        if hook is not None:
            hook()
        select = selected(dst)
        accs = []
        for field in fields:
            src = field[...]
            acc = (jnp.zeros((3, *TILE), jnp.float32),) * 2
            for n, (_, by) in enumerate(X_HOPS):
                acc = times(acc, dst, n, along_x(g, by, src))
            for mu, axis in enumerate(AXES):
                for kind in range(2):
                    acc = times(acc, dst, 4 + 4 * mu + kind, turn(g, axis, kind, src, select))
            accs.append(acc)
        if border_hook is not None:
            border_hook()
        per_axis = 2 * len(fields)
        for axis, mu in (("gz", 1), ("gy", 2), ("ta", 0)):
            for c in copies[per_axis * mu : per_axis * (mu + 1)]:
                c.wait_recv()
            for f in range(len(fields)):
                ahead, behind = halo[slot, f, mu, 0], halo[slot, f, mu, 1]
                for kind in range(2):
                    v = across(g, axis, kind, ahead, behind, select)
                    accs[f] = times(accs[f], dst, 6 + 4 * mu + kind, v)
        for c in copies:
            c.wait_send()
        return [jnp.concatenate(acc, axis=0) for acc in accs]

    def first_half(fields, hook=None, border_hook=None):
        for f, value in enumerate(half(fields, 1, hook, border_hook)):
            odd_f[f] = value

    def second_half(fields, diagonal, hook=None, border_hook=None):
        odds = [odd_f.at[f] for f in range(len(fields))]
        values = half(odds, 0, hook, border_hook)
        return [diagonal * v[...] - d for v, d in zip(fields, values)]

    def stage_copies(blk, stage, place_of):
        copies = []
        for n, (device, place) in enumerate(peers(stage)):
            spot = my_place(stage) if place_of == "mine" else place
            copies.append(
                pltpu.make_async_remote_copy(
                    src_ref=row,
                    dst_ref=sums.at[stage, blk, spot],
                    send_sem=sum_send.at[n],
                    recv_sem=sum_recv.at[stage, blk, spot],
                    device_id=device,
                    device_id_type=mesh_id,
                )
            )
        return copies

    def stage_start(blk, stage, line):
        row[...] = line
        sums[stage, blk, my_place(stage)] = line
        for c in stage_copies(blk, stage, "mine"):
            c.start()

    def stage_end(blk, stage):
        for c in stage_copies(blk, stage, "theirs"):
            c.wait_send()
            c.wait_recv()
        return jnp.sum(sums[stage, blk], axis=0)

    lane = lax.broadcasted_iota(jnp.int32, (1, 128), 1)

    def local_dots():
        r, w, q = vec[0], vec[1], vec[2]
        m, v = prev[0], prev[1]
        pairs = ((r, r), (r, w), (w, w), (w, q), (r, m), (w, m), (w, v), (m, m), (m, v))
        line = jnp.zeros((1, 128), jnp.float32)
        for n, (a, b) in enumerate(pairs):
            line = line + jnp.where(lane == n, jnp.sum(jnp.sum(a * b, axis=0)), 0.0)
        return line

    def coefficients(line):
        rr, rw, ww, wq, rm, wm, wv, mm, mv = (
            jnp.broadcast_to(jnp.sum(jnp.where(lane == n, line, 0.0)), TILE) for n in range(DOTS)
        )
        c = shift[...]
        step = rr / (rw + c * rr)
        scale = 1.0 / (1.0 - step * rr * kept[...])
        u, f, h = scale * (1.0 - step * c), -scale * step, 1.0 - scale
        rr1 = u * u * rr + f * f * ww + h * h * mm + 2.0 * (u * f * rw + u * h * rm + f * h * wm)
        rw1 = u * u * rw + f * f * wq + h * h * mv + 2.0 * (u * f * ww + u * h * wm + f * h * wv)
        mean1 = (rw1 + c * rr1) / rr1
        step1 = 1.0 / mean1
        scale1 = 1.0 / (1.0 - step1 * rr1 / (step * rr * scale))
        u1, f1, h1 = scale1 * (1.0 - step1 * c), -scale1 * step1, 1.0 - scale1
        kept[...] = 1.0 / (step1 * rr1 * scale1)
        return (step, scale, u, f, h), (step1, scale1, u1, f1, h1), mean1

    def early_update(line):
        (step, scale, u, f, h), (step1, scale1, u1, f1, h1), mean1 = coefficients(line)
        first = [u * vec[k] + f * vec[k + 1] + h * prev[k] for k in range(3)]
        second = [u1 * first[k] + f1 * first[k + 1] + h1 * vec[k] for k in range(2)]
        x, x0 = xs[0], xs[1]
        x1 = scale * (x + step * vec[0]) + h * x0
        xs[1] = x1
        xs[0] = scale1 * (x1 + step1 * first[0]) + h1 * x
        d = mean1 - shift[...]
        shift[...] = mean1
        half_first3 = u * vec[3] + h * prev[3]
        half_second2 = u1 * first[2] + h1 * vec[2]
        return d, f, f1, first, second, half_first3, half_second2

    def late_update(parts, fourth):
        d, f, f1, first, second, half_first3, half_second2 = parts
        first = first + [half_first3 + f * fourth]
        second = second + [half_second2 + f1 * first[3]]
        for stack, place in ((second, vec), (first, prev)):
            for k in range(len(stack)):
                place[k] = stack[0]
                stack = [b - d * a for a, b in zip(stack, stack[1:])]

    def last_update(line):
        (step, scale, u, f, h), (step1, scale1, u1, f1, h1), _ = coefficients(line)
        c = shift[...]
        r, w, q, m, v = vec[0], vec[1], vec[2], prev[0], prev[1]
        x, x0, ax, ax0 = xs[0], xs[1], images[0], images[1]
        r1 = u * r + f * w + h * m
        x1 = scale * (x + step * r) + h * x0
        x_out[...] = scale1 * (x1 + step1 * r1) + h1 * x
        ar = w + c * r
        ar1 = u * ar + f * (q + c * w) + h * (v + c * m)
        ax1 = scale * (ax + step * ar) + h * ax0
        t_out[...] = src_b[...] - (scale1 * (ax1 + step1 * ar1) + h1 * ax)

    loads[0].wait()
    vec[0] = src_b[...]
    prev[...] = jnp.zeros_like(prev)
    xs[...] = jnp.zeros_like(xs)
    kept[...] = jnp.zeros_like(kept)
    shift[...] = jnp.zeros_like(shift)

    def first_links():
        loads[1].wait()
        loads[2].wait()
        for copies in rim:
            for c in copies:
                c.start()
        local_matrices(1)

    def second_borders():
        border_matrices(0)
        for copies in rim:
            for c in copies:
                c.wait_send()

    first_half([src_b], first_links, lambda: border_matrices(1))
    (vec[1],) = second_half([src_b], MASS, lambda: local_matrices(0), second_borders)
    first_half([vec.at[1]])
    (vec[2],) = second_half([vec.at[1]], MASS)

    def block(blk, carry):
        diagonal = MASS - shift[...]
        first_half([vec.at[2]], lambda: stage_start(blk, 0, local_dots()))
        (vec[3],) = second_half(
            [vec.at[2]], diagonal, lambda: stage_start(blk, 1, stage_end(blk, 0))
        )
        first_half([vec.at[3]])
        parts = []
        (fourth,) = second_half(
            [vec.at[3]], diagonal, lambda: parts.extend(early_update(stage_end(blk, 1)))
        )
        late_update(parts, fourth)
        return carry

    lax.fori_loop(0, BLOCKS - 1, block, 0)
    last = BLOCKS - 1
    both = [xs.at[0], xs.at[1]]
    first_half(both, lambda: stage_start(last, 0, local_dots()))
    images[0], images[1] = second_half(
        both, MASS, lambda: stage_start(last, 1, stage_end(last, 0))
    )
    last_update(stage_end(last, 1))


def per_device(source, fat_links, long_links):
    f32 = jnp.float32
    field = (6, *TILE)
    dma = pltpu.SemaphoreType.DMA
    fat = fat_links.reshape(2, 4, 18, *TILE)
    long = long_links.reshape(2, 4, 18, *TILE)
    vmem = pl.BlockSpec(memory_space=pltpu.VMEM)
    hbm = pl.BlockSpec(memory_space=pltpu.HBM)
    x, t = pl.pallas_call(
        kernel,
        out_shape=(jax.ShapeDtypeStruct(field, f32), jax.ShapeDtypeStruct(field, f32)),
        in_specs=[hbm] * 3,
        out_specs=(vmem, vmem),
        scratch_shapes=[
            pltpu.VMEM(fat.shape, fat.dtype),
            pltpu.VMEM(long.shape, long.dtype),
            pltpu.VMEM(field, f32),
            pltpu.VMEM((4, *field), f32),
            pltpu.VMEM((4, *field), f32),
            pltpu.VMEM((2, *field), f32),
            pltpu.VMEM((2, *field), f32),
            pltpu.VMEM((2, *field), f32),
            pltpu.VMEM((2, 16, 18, *TILE), f32),
            pltpu.VMEM((2, 2, 3, 2, *field), f32),
            pltpu.VMEM((2, 3, 2, 18, *TILE), jnp.bfloat16),
            pltpu.VMEM((1, 128), f32),
            pltpu.VMEM((2, BLOCKS, MEMBERS, 1, 128), f32),
            pltpu.VMEM(TILE, f32),
            pltpu.VMEM(TILE, f32),
            dma((3,)),
            dma((2, 2, 3, 2)),
            dma((2, 2, 3, 2)),
            dma((2, 3, 2)),
            dma((2, 3, 2)),
            dma((MEMBERS - 1,)),
            dma((2, BLOCKS, MEMBERS)),
        ],
        compiler_params=pltpu.CompilerParams(
            collective_id=0, has_side_effects=True
        ),
    )(source.reshape(field), fat, long)
    return x.reshape(source.shape), t.reshape(source.shape)


def solution(mesh):
    field = P(None, None, "ta", "gz", "gy")
    links = P(None, None, None, None, None, "ta", "gz", "gy")
    return jax.shard_map(
        per_device,
        mesh=mesh,
        in_specs=(field, links, links),
        out_specs=(field, field),
        check_vma=False,
    )
```

```python
import jax
import jax.numpy as jnp
from jax import lax
from jax.experimental import pallas as pl
from jax.experimental.pallas import tpu as pltpu
from jax.sharding import PartitionSpec as P

NX = 32
BLOCKS = 4
MASS = 0.1
AXES = ("ta", "gz", "gy")
SIZES = {"ta": 4, "gz": 8, "gy": 8}
MEMBERS = 16
DOTS = 9
TILE = (8, 128)


def iota(axis):
    return lax.broadcasted_iota(jnp.int32, TILE, axis)


class Grid:
    def __init__(self):
        sub, lane = iota(0), iota(1)
        self.row, self.z = sub // 4, sub % 4
        self.lane, self.x = lane, lane % NX
        self.odd = (self.z + lane // NX + self.x) % 2 == 1


def roll(field, shift, axis):
    return pltpu.roll(field, shift % TILE[axis], axis + 1)


def turn(g, axis, kind, field, select):
    if axis == "ta":
        rolled = roll(field, 4, 0)
        return jnp.where(select, rolled, field) if kind == 0 else jnp.where(select, field, rolled)
    if axis == "gz":
        if kind == 0:
            return jnp.where(g.z < 3, roll(field, -1, 0), roll(field, 3, 0))
        return jnp.where(g.z > 0, roll(field, 1, 0), roll(field, -3, 0))
    return roll(field, -NX if kind == 0 else NX, 1)


def across(g, axis, kind, ahead, behind, select):
    if axis == "ta":
        rolled = roll(jnp.where(g.row == 0, ahead, behind), 4, 0)
        return jnp.where(select, rolled, behind) if kind == 0 else jnp.where(select, ahead, rolled)
    if axis == "gz":
        mixed = jnp.where(g.z == 0 if kind == 0 else g.z < 3, ahead, behind)
    else:
        mixed = jnp.where(g.lane < (NX if kind == 0 else 3 * NX), ahead, behind)
    return turn(g, axis, kind, mixed, select)


def inside(g, axis, kind, select):
    if axis == "ta":
        unselected = jnp.logical_not(select)
        first = g.row == 0
        return jnp.logical_or(unselected, first) if kind == 0 else jnp.logical_and(unselected, first)
    if axis == "gz":
        return g.z < 3 if kind == 0 else g.z == 0
    return g.lane < (3 * NX if kind == 0 else NX)


def along_x(g, by, field):
    if by > 0:
        return jnp.where(g.x < NX - by, roll(field, -by, 1), roll(field, NX - by, 1))
    return jnp.where(g.x >= -by, roll(field, -by, 1), roll(field, -by - NX, 1))


def kernel(
    b_hbm,
    fat_hbm,
    long_hbm,
    x_out,
    t_out,
    fat_ref,
    long_ref,
    src_b,
    vec,
    prev,
    xs,
    images,
    odd_f,
    mats,
    products,
    halo,
    rims,
    row,
    sums,
    kept,
    shift,
    load,
    halo_send,
    halo_recv,
    rim_send,
    rim_recv,
    sum_send,
    sum_recv,
):
    g = Grid()
    me = {a: lax.axis_index(a) for a in AXES}
    mesh_id = pl.DeviceIdType.MESH

    def at(axis, by):
        return {axis: lax.rem(me[axis] + (by % SIZES[axis]), SIZES[axis])}

    low, high = lax.rem(me["ta"], 2), me["ta"] // 2
    groups = (("gz", low, me["ta"] + 1 - 2 * low), ("gy", high, 3 - me["ta"]))

    def peers(stage):
        axis, bit, partner = groups[stage]
        for by in range(SIZES[axis]):
            there = lax.rem(me[axis] + by, SIZES[axis])
            if by:
                yield {axis: there}, 2 * there + bit
            yield {axis: there, "ta": partner}, 2 * there + 1 - bit

    def my_place(stage):
        axis, bit, _ = groups[stage]
        return 2 * me[axis] + bit

    barrier = pltpu.get_barrier_semaphore()
    for axis in AXES:
        for by in (-1, 1):
            pl.semaphore_signal(barrier, inc=1, device_id=at(axis, by), device_id_type=mesh_id)
    loads = [
        pltpu.make_async_copy(a, c, load.at[n])
        for n, (a, c) in enumerate(
            [(b_hbm, src_b)]
            + [(a.at[p], c.at[p]) for p in (0, 1) for a, c in ((fat_hbm, fat_ref), (long_hbm, long_ref))]
        )
    ]
    for c in loads:
        c.start()
    pl.semaphore_wait(barrier, 2 * len(AXES))

    def halo_copies(fields, slot):
        copies = []
        for n, axis in enumerate(AXES):
            for side, by in enumerate((-1, 1)):
                for f, src in enumerate(fields):
                    copies.append(
                        pltpu.make_async_remote_copy(
                            src_ref=src,
                            dst_ref=halo.at[slot, f, n, side],
                            send_sem=halo_send.at[slot, f, n, side],
                            recv_sem=halo_recv.at[slot, f, n, side],
                            device_id=at(axis, by),
                            device_id_type=mesh_id,
                        )
                    )
        return copies

    def rim_copies(p):
        copies = []
        for n, axis in enumerate(AXES):
            for kind, links in enumerate((fat_ref, long_ref)):
                copies.append(
                    pltpu.make_async_remote_copy(
                        src_ref=links.at[p, n],
                        dst_ref=rims.at[p, n, kind],
                        send_sem=rim_send.at[p, n, kind],
                        recv_sem=rim_recv.at[p, n, kind],
                        device_id=at(axis, 1),
                        device_id_type=mesh_id,
                    )
                )
        return copies

    def selected(dst):
        return g.odd if dst == 0 else jnp.logical_not(g.odd)

    rim = [rim_copies(0), rim_copies(1)]

    def plain(links, p, mu):
        columns = [links[p, mu, pl.ds(9 * part + j, 3, stride=3)] for part in (0, 1) for j in range(3)]
        return jnp.concatenate(columns, axis=0).astype(jnp.float32)

    def minus_adjoint(links):
        links = links.astype(jnp.float32)
        return jnp.concatenate([-links[:9], links[9:]], axis=0)

    kinds = (fat_ref, long_ref)
    X_HOPS = ((0, 1), (1, 3), (0, -1), (1, -3))

    def local_matrices(dst):
        select = selected(dst)
        for n, (kind, by) in enumerate(X_HOPS):
            if by > 0:
                mats[dst, n] = plain(kinds[kind], dst, 3)
            else:
                links = kinds[kind][1 - dst, 3].astype(jnp.float32)
                mats[dst, n] = minus_adjoint(along_x(g, by, links))
        for mu, axis in enumerate(AXES):
            for kind in range(2):
                links = kinds[1 - kind][1 - dst, mu].astype(jnp.float32)
                mats[dst, 4 + 4 * mu + kind] = jnp.where(
                    inside(g, axis, kind, select),
                    plain(kinds[kind], dst, mu),
                    minus_adjoint(turn(g, axis, kind, links, select)),
                )

    def border_matrices(dst):
        select = selected(dst)
        for mu, axis in enumerate(AXES):
            for kind in range(2):
                rim[1 - dst][2 * mu + 1 - kind].wait_recv()
                links = rims[1 - dst, mu, 1 - kind].astype(jnp.float32)
                mats[dst, 6 + 4 * mu + kind] = jnp.where(
                    inside(g, axis, kind, select),
                    minus_adjoint(turn(g, axis, kind, links, select)),
                    plain(kinds[kind], dst, mu),
                )

    def times(acc, dst, k, v):
        re, im = acc
        vr, vi = v[:3], v[3:]
        for j in range(3):
            mr, mi = mats[dst, k, pl.ds(3 * j, 3)], mats[dst, k, pl.ds(9 + 3 * j, 3)]
            re = re + mr * vr[j][None] - mi * vi[j][None]
            im = im + mr * vi[j][None] + mi * vr[j][None]
        return re, im

    def local_products(src, dst, select):
        acc = (jnp.zeros((3, *TILE), jnp.float32),) * 2
        for n, (_, by) in enumerate(X_HOPS):
            acc = times(acc, dst, n, along_x(g, by, src))
        for mu, axis in enumerate(AXES):
            for kind in range(2):
                acc = times(acc, dst, 4 + 4 * mu + kind, turn(g, axis, kind, src, select))
        return acc

    def half(fields, dst, hook=None, border_hook=None):
        slot = dst
        copies = halo_copies(fields, slot)
        for c in copies:
            c.start()
        if hook is not None:
            hook()
        select = selected(dst)
        accs = [local_products(field[...], dst, select) for field in fields]
        if border_hook is not None:
            border_hook()
        per_axis = 2 * len(fields)
        for axis, mu in (("gz", 1), ("gy", 2), ("ta", 0)):
            for c in copies[per_axis * mu : per_axis * (mu + 1)]:
                c.wait_recv()
            for f in range(len(fields)):
                ahead, behind = halo[slot, f, mu, 0], halo[slot, f, mu, 1]
                for kind in range(2):
                    v = across(g, axis, kind, ahead, behind, select)
                    accs[f] = times(accs[f], dst, 6 + 4 * mu + kind, v)
        for c in copies:
            c.wait_send()
        return [jnp.concatenate(acc, axis=0) for acc in accs]

    def first_half(fields, hook=None, border_hook=None):
        for f, value in enumerate(half(fields, 1, hook, border_hook)):
            odd_f[f] = value

    def second_half(fields, diagonal, hook=None, border_hook=None):
        odds = [odd_f.at[f] for f in range(len(fields))]
        values = half(odds, 0, hook, border_hook)
        return [diagonal * v[...] - d for v, d in zip(fields, values)]

    def stage_copies(blk, stage, place_of):
        copies = []
        for n, (device, place) in enumerate(peers(stage)):
            spot = my_place(stage) if place_of == "mine" else place
            copies.append(
                pltpu.make_async_remote_copy(
                    src_ref=row,
                    dst_ref=sums.at[stage, blk, spot],
                    send_sem=sum_send.at[n],
                    recv_sem=sum_recv.at[stage, blk, spot],
                    device_id=device,
                    device_id_type=mesh_id,
                )
            )
        return copies

    def stage_start(blk, stage, line):
        row[...] = line
        sums[stage, blk, my_place(stage)] = line
        for c in stage_copies(blk, stage, "mine"):
            c.start()

    def stage_end(blk, stage):
        for c in stage_copies(blk, stage, "theirs"):
            c.wait_send()
            c.wait_recv()
        return jnp.sum(sums[stage, blk], axis=0)

    lane = lax.broadcasted_iota(jnp.int32, (1, 128), 1)

    def local_dots():
        r, w, q = vec[0], vec[1], vec[2]
        m, v = prev[0], prev[1]
        pairs = ((r, r), (r, w), (w, w), (w, q), (r, m), (w, m), (w, v), (m, m), (m, v))
        line = jnp.zeros((1, 128), jnp.float32)
        for n, (a, b) in enumerate(pairs):
            line = line + jnp.where(lane == n, jnp.sum(jnp.sum(a * b, axis=0)), 0.0)
        return line

    def coefficients(line):
        rr, rw, ww, wq, rm, wm, wv, mm, mv = (
            jnp.broadcast_to(jnp.sum(jnp.where(lane == n, line, 0.0)), TILE) for n in range(DOTS)
        )
        c = shift[...]
        step = rr / (rw + c * rr)
        scale = 1.0 / (1.0 - step * rr * kept[...])
        u, f, h = scale * (1.0 - step * c), -scale * step, 1.0 - scale
        rr1 = u * u * rr + f * f * ww + h * h * mm + 2.0 * (u * f * rw + u * h * rm + f * h * wm)
        rw1 = u * u * rw + f * f * wq + h * h * mv + 2.0 * (u * f * ww + u * h * wm + f * h * wv)
        mean1 = (rw1 + c * rr1) / rr1
        step1 = 1.0 / mean1
        scale1 = 1.0 / (1.0 - step1 * rr1 / (step * rr * scale))
        u1, f1, h1 = scale1 * (1.0 - step1 * c), -scale1 * step1, 1.0 - scale1
        kept[...] = 1.0 / (step1 * rr1 * scale1)
        return (step, scale, u, f, h), (step1, scale1, u1, f1, h1), mean1

    def early_update(line):
        (step, scale, u, f, h), (step1, scale1, u1, f1, h1), mean1 = coefficients(line)
        first = [u * vec[k] + f * vec[k + 1] + h * prev[k] for k in range(3)]
        second = [u1 * first[k] + f1 * first[k + 1] + h1 * vec[k] for k in range(2)]
        x, x0 = xs[0], xs[1]
        x1 = scale * (x + step * vec[0]) + h * x0
        xs[1] = x1
        xs[0] = scale1 * (x1 + step1 * first[0]) + h1 * x
        d = mean1 - shift[...]
        shift[...] = mean1
        half_first3 = u * vec[3] + h * prev[3]
        half_second2 = u1 * first[2] + h1 * vec[2]
        return d, f, f1, first, second, half_first3, half_second2

    def late_update(parts, fourth):
        d, f, f1, first, second, half_first3, half_second2 = parts
        first = first + [half_first3 + f * fourth]
        second = second + [half_second2 + f1 * first[3]]
        for stack, place in ((second, vec), (first, prev)):
            for k in range(len(stack)):
                place[k] = stack[0]
                stack = [b - d * a for a, b in zip(stack, stack[1:])]

    def last_update(line):
        (step, scale, u, f, h), (step1, scale1, u1, f1, h1), _ = coefficients(line)
        c = shift[...]
        r, w, q, m, v = vec[0], vec[1], vec[2], prev[0], prev[1]
        x, x0, ax, ax0 = xs[0], xs[1], images[0], images[1]
        r1 = u * r + f * w + h * m
        x1 = scale * (x + step * r) + h * x0
        x_out[...] = scale1 * (x1 + step1 * r1) + h1 * x
        ar = w + c * r
        ar1 = u * ar + f * (q + c * w) + h * (v + c * m)
        ax1 = scale * (ax + step * ar) + h * ax0
        t_out[...] = src_b[...] - (scale1 * (ax1 + step1 * ar1) + h1 * ax)

    loads[0].wait()
    vec[0] = src_b[...]
    prev[...] = jnp.zeros_like(prev)
    xs[...] = jnp.zeros_like(xs)
    kept[...] = jnp.zeros_like(kept)
    shift[...] = jnp.zeros_like(shift)

    def to_neighbour(src, field, n, side):
        return pltpu.make_async_remote_copy(
            src_ref=src,
            dst_ref=halo.at[1, field, n, side],
            send_sem=halo_send.at[1, field, n, side],
            recv_sem=halo_recv.at[1, field, n, side],
            device_id=at(AXES[n], 2 * side - 1),
            device_id_type=mesh_id,
        )

    def adjoint_product(links, mu, src):
        re = im = jnp.zeros((3, *TILE), jnp.float32)
        for i in range(3):
            lr = links[0, mu, pl.ds(3 * i, 3)].astype(jnp.float32)
            li = links[0, mu, pl.ds(9 + 3 * i, 3)].astype(jnp.float32)
            vr, vi = src[i][None], src[3 + i][None]
            re = re - lr * vr - li * vi
            im = im - lr * vi + li * vr
        return jnp.concatenate([re, im], axis=0)

    def opening_half():
        select = selected(1)
        forth = [to_neighbour(src_b, 0, n, 0) for n in range(3)]
        for c in forth:
            c.start()
        loads[1].wait()
        loads[2].wait()
        src = src_b[...]
        back = []
        for n in range(3):
            for kind in range(2):
                products[n, kind] = adjoint_product(kinds[1 - kind], n, src)
                back.append(to_neighbour(products.at[n, kind], kind, n, 1))
        for c in back:
            c.start()
        loads[3].wait()
        loads[4].wait()
        for p in (1, 0):
            for c in rim[p]:
                c.start()
        local_matrices(1)
        for mu, axis in enumerate(AXES):
            for kind in range(2):
                links = plain(kinds[kind], 1, mu)
                mats[1, 6 + 4 * mu + kind] = jnp.where(
                    inside(g, axis, kind, select), jnp.zeros_like(links), links
                )
        acc = local_products(src, 1, select)
        for axis, mu in (("gz", 1), ("gy", 2), ("ta", 0)):
            forth[mu].wait_recv()
            ahead = halo[1, 0, mu, 0]
            for kind in range(2):
                v = across(g, axis, kind, ahead, ahead, select)
                re, im = times(acc, 1, 6 + 4 * mu + kind, v)
                back[2 * mu + kind].wait_recv()
                made = turn(g, axis, kind, halo[1, kind, mu, 1], select)
                made = jnp.where(inside(g, axis, kind, select), made, 0.0)
                acc = (re + made[:3], im + made[3:])
        odd_f[0] = jnp.concatenate(acc, axis=0)
        for c in forth + back:
            c.wait_send()

    def link_sends_end():
        for copies in rim:
            for c in copies:
                c.wait_send()

    opening_half()
    (vec[1],) = second_half([src_b], MASS, lambda: local_matrices(0), lambda: border_matrices(0))
    link_sends_end()
    first_half([vec.at[1]], None, lambda: border_matrices(1))
    (vec[2],) = second_half([vec.at[1]], MASS)

    def block(blk, carry):
        diagonal = MASS - shift[...]
        first_half([vec.at[2]], lambda: stage_start(blk, 0, local_dots()))
        (vec[3],) = second_half(
            [vec.at[2]], diagonal, lambda: stage_start(blk, 1, stage_end(blk, 0))
        )
        first_half([vec.at[3]])
        parts = []
        (fourth,) = second_half(
            [vec.at[3]], diagonal, lambda: parts.extend(early_update(stage_end(blk, 1)))
        )
        late_update(parts, fourth)
        return carry

    lax.fori_loop(0, BLOCKS - 1, block, 0)
    last = BLOCKS - 1
    both = [xs.at[0], xs.at[1]]
    first_half(both, lambda: stage_start(last, 0, local_dots()))
    images[0], images[1] = second_half(
        both, MASS, lambda: stage_start(last, 1, stage_end(last, 0))
    )
    last_update(stage_end(last, 1))


def per_device(source, fat_links, long_links):
    f32 = jnp.float32
    field = (6, *TILE)
    dma = pltpu.SemaphoreType.DMA
    fat = fat_links.reshape(2, 4, 18, *TILE)
    long = long_links.reshape(2, 4, 18, *TILE)
    vmem = pl.BlockSpec(memory_space=pltpu.VMEM)
    hbm = pl.BlockSpec(memory_space=pltpu.HBM)
    x, t = pl.pallas_call(
        kernel,
        out_shape=(pltpu.VMEM(field, f32), pltpu.VMEM(field, f32)),
        in_specs=[hbm] * 3,
        out_specs=(vmem, vmem),
        scratch_shapes=[
            pltpu.VMEM(fat.shape, fat.dtype),
            pltpu.VMEM(long.shape, long.dtype),
            pltpu.VMEM(field, f32),
            pltpu.VMEM((4, *field), f32),
            pltpu.VMEM((4, *field), f32),
            pltpu.VMEM((2, *field), f32),
            pltpu.VMEM((2, *field), f32),
            pltpu.VMEM((2, *field), f32),
            pltpu.VMEM((2, 16, 18, *TILE), f32),
            pltpu.VMEM((3, 2, *field), f32),
            pltpu.VMEM((2, 2, 3, 2, *field), f32),
            pltpu.VMEM((2, 3, 2, 18, *TILE), jnp.bfloat16),
            pltpu.VMEM((1, 128), f32),
            pltpu.VMEM((2, BLOCKS, MEMBERS, 1, 128), f32),
            pltpu.VMEM(TILE, f32),
            pltpu.VMEM(TILE, f32),
            dma((5,)),
            dma((2, 2, 3, 2)),
            dma((2, 2, 3, 2)),
            dma((2, 3, 2)),
            dma((2, 3, 2)),
            dma((MEMBERS - 1,)),
            dma((2, BLOCKS, MEMBERS)),
        ],
        compiler_params=pltpu.CompilerParams(
            collective_id=0, has_side_effects=True
        ),
    )(source.reshape(field), fat, long)
    return x.reshape(source.shape), t.reshape(source.shape)


def solution(mesh):
    field = P(None, None, "ta", "gz", "gy")
    links = P(None, None, None, None, None, "ta", "gz", "gy")
    return jax.shard_map(
        per_device,
        mesh=mesh,
        in_specs=(field, links, links),
        out_specs=(field, field),
        check_vma=False,
    )
```

```python
import jax
import jax.numpy as jnp
from jax import lax
from jax.experimental import pallas as pl
from jax.experimental.pallas import tpu as pltpu
from jax.sharding import PartitionSpec as P

NX = 32
BLOCKS = 4
MASS = 0.1
AXES = ("ta", "gz", "gy")
SIZES = {"ta": 4, "gz": 8, "gy": 8}
MEMBERS = 16
DOTS = 9
TILE = (8, 128)


def iota(axis):
    return lax.broadcasted_iota(jnp.int32, TILE, axis)


class Grid:
    def __init__(self):
        sub, lane = iota(0), iota(1)
        self.row, self.z = sub // 4, sub % 4
        self.lane, self.x = lane, lane % NX
        self.odd = (self.z + lane // NX + self.x) % 2 == 1


def roll(field, shift, axis):
    return pltpu.roll(field, shift % TILE[axis], axis + 1)


def turn(g, axis, kind, field, select):
    if axis == "ta":
        rolled = roll(field, 4, 0)
        return jnp.where(select, rolled, field) if kind == 0 else jnp.where(select, field, rolled)
    if axis == "gz":
        if kind == 0:
            return jnp.where(g.z < 3, roll(field, -1, 0), roll(field, 3, 0))
        return jnp.where(g.z > 0, roll(field, 1, 0), roll(field, -3, 0))
    return roll(field, -NX if kind == 0 else NX, 1)


def across(g, axis, kind, ahead, behind, select):
    if axis == "ta":
        rolled = roll(jnp.where(g.row == 0, ahead, behind), 4, 0)
        return jnp.where(select, rolled, behind) if kind == 0 else jnp.where(select, ahead, rolled)
    if axis == "gz":
        mixed = jnp.where(g.z == 0 if kind == 0 else g.z < 3, ahead, behind)
    else:
        mixed = jnp.where(g.lane < (NX if kind == 0 else 3 * NX), ahead, behind)
    return turn(g, axis, kind, mixed, select)


def inside(g, axis, kind, select):
    if axis == "ta":
        unselected = jnp.logical_not(select)
        first = g.row == 0
        return jnp.logical_or(unselected, first) if kind == 0 else jnp.logical_and(unselected, first)
    if axis == "gz":
        return g.z < 3 if kind == 0 else g.z == 0
    return g.lane < (3 * NX if kind == 0 else NX)


def along_x(g, by, field):
    if by > 0:
        return jnp.where(g.x < NX - by, roll(field, -by, 1), roll(field, NX - by, 1))
    return jnp.where(g.x >= -by, roll(field, -by, 1), roll(field, -by - NX, 1))


def kernel(
    b_hbm,
    fat_hbm,
    long_hbm,
    x_out,
    t_out,
    fat_ref,
    long_ref,
    src_b,
    vec,
    prev,
    xs,
    images,
    odd_f,
    mats,
    products,
    halo,
    rims,
    row,
    sums,
    kept,
    shift,
    load,
    halo_send,
    halo_recv,
    rim_send,
    rim_recv,
    sum_send,
    sum_recv,
):
    g = Grid()
    me = {a: lax.axis_index(a) for a in AXES}
    mesh_id = pl.DeviceIdType.MESH

    def at(axis, by):
        return {axis: lax.rem(me[axis] + (by % SIZES[axis]), SIZES[axis])}

    low, high = lax.rem(me["ta"], 2), me["ta"] // 2
    groups = (("gz", low, me["ta"] + 1 - 2 * low), ("gy", high, 3 - me["ta"]))

    def peers(stage):
        axis, bit, partner = groups[stage]
        for by in range(SIZES[axis]):
            there = lax.rem(me[axis] + by, SIZES[axis])
            if by:
                yield {axis: there}, 2 * there + bit
            yield {axis: there, "ta": partner}, 2 * there + 1 - bit

    def my_place(stage):
        axis, bit, _ = groups[stage]
        return 2 * me[axis] + bit

    barrier = pltpu.get_barrier_semaphore()
    for axis in AXES:
        for by in (-1, 1):
            pl.semaphore_signal(barrier, inc=1, device_id=at(axis, by), device_id_type=mesh_id)
    loads = [
        pltpu.make_async_copy(a, c, load.at[n])
        for n, (a, c) in enumerate(
            [(b_hbm, src_b)]
            + [(a.at[p], c.at[p]) for p in (0, 1) for a, c in ((fat_hbm, fat_ref), (long_hbm, long_ref))]
        )
    ]
    for c in loads:
        c.start()
    pl.semaphore_wait(barrier, 2 * len(AXES))

    def halo_copies(fields, slot, base=0):
        copies = []
        for n, axis in enumerate(AXES):
            for side, by in enumerate((-1, 1)):
                for f, src in enumerate(fields, base):
                    copies.append(
                        pltpu.make_async_remote_copy(
                            src_ref=src,
                            dst_ref=halo.at[slot, f, n, side],
                            send_sem=halo_send.at[slot, f, n, side],
                            recv_sem=halo_recv.at[slot, f, n, side],
                            device_id=at(axis, by),
                            device_id_type=mesh_id,
                        )
                    )
        return copies

    def rim_copies(p):
        copies = []
        for n, axis in enumerate(AXES):
            for kind, links in enumerate((fat_ref, long_ref)):
                copies.append(
                    pltpu.make_async_remote_copy(
                        src_ref=links.at[p, n],
                        dst_ref=rims.at[p, n, kind],
                        send_sem=rim_send.at[p, n, kind],
                        recv_sem=rim_recv.at[p, n, kind],
                        device_id=at(axis, 1),
                        device_id_type=mesh_id,
                    )
                )
        return copies

    def selected(dst):
        return g.odd if dst == 0 else jnp.logical_not(g.odd)

    rim = [rim_copies(0), rim_copies(1)]

    def plain(links, p, mu):
        columns = [links[p, mu, pl.ds(9 * part + j, 3, stride=3)] for part in (0, 1) for j in range(3)]
        return jnp.concatenate(columns, axis=0).astype(jnp.float32)

    def minus_adjoint(links):
        links = links.astype(jnp.float32)
        return jnp.concatenate([-links[:9], links[9:]], axis=0)

    kinds = (fat_ref, long_ref)
    X_HOPS = ((0, 1), (1, 3), (0, -1), (1, -3))

    def local_matrices(dst):
        select = selected(dst)
        for n, (kind, by) in enumerate(X_HOPS):
            if by > 0:
                mats[dst, n] = plain(kinds[kind], dst, 3)
            else:
                links = kinds[kind][1 - dst, 3].astype(jnp.float32)
                mats[dst, n] = minus_adjoint(along_x(g, by, links))
        for mu, axis in enumerate(AXES):
            for kind in range(2):
                links = kinds[1 - kind][1 - dst, mu].astype(jnp.float32)
                mats[dst, 4 + 4 * mu + kind] = jnp.where(
                    inside(g, axis, kind, select),
                    plain(kinds[kind], dst, mu),
                    minus_adjoint(turn(g, axis, kind, links, select)),
                )

    def border_matrices(dst):
        select = selected(dst)
        for mu, axis in enumerate(AXES):
            for kind in range(2):
                rim[1 - dst][2 * mu + 1 - kind].wait_recv()
                links = rims[1 - dst, mu, 1 - kind].astype(jnp.float32)
                mats[dst, 6 + 4 * mu + kind] = jnp.where(
                    inside(g, axis, kind, select),
                    minus_adjoint(turn(g, axis, kind, links, select)),
                    plain(kinds[kind], dst, mu),
                )

    def times(acc, dst, k, v):
        re, im = acc
        vr, vi = v[:3], v[3:]
        for j in range(3):
            mr, mi = mats[dst, k, pl.ds(3 * j, 3)], mats[dst, k, pl.ds(9 + 3 * j, 3)]
            re = re + mr * vr[j][None] - mi * vi[j][None]
            im = im + mr * vi[j][None] + mi * vr[j][None]
        return re, im

    def local_products(src, dst, select):
        acc = (jnp.zeros((3, *TILE), jnp.float32),) * 2
        for n, (_, by) in enumerate(X_HOPS):
            acc = times(acc, dst, n, along_x(g, by, src))
        for mu, axis in enumerate(AXES):
            for kind in range(2):
                acc = times(acc, dst, 4 + 4 * mu + kind, turn(g, axis, kind, src, select))
        return acc

    def border_products(accs, copies, dst, select, base=0):
        per_axis = 2 * len(accs)
        for axis, mu in (("gz", 1), ("gy", 2), ("ta", 0)):
            for c in copies[per_axis * mu : per_axis * (mu + 1)]:
                c.wait_recv()
            for f in range(len(accs)):
                ahead, behind = halo[dst, base + f, mu, 0], halo[dst, base + f, mu, 1]
                for kind in range(2):
                    v = across(g, axis, kind, ahead, behind, select)
                    accs[f] = times(accs[f], dst, 6 + 4 * mu + kind, v)
        return [jnp.concatenate(acc, axis=0) for acc in accs]

    def half(fields, dst, hook=None, border_hook=None, base=0):
        copies = halo_copies(fields, dst, base)
        for c in copies:
            c.start()
        if hook is not None:
            hook()
        select = selected(dst)
        accs = [local_products(field[...], dst, select) for field in fields]
        if border_hook is not None:
            border_hook()
        out = border_products(accs, copies, dst, select, base)
        for c in copies:
            c.wait_send()
        return out

    def two_halves(fields, others, hook):
        copies, more = halo_copies(fields, 0), halo_copies(others, 1, 1)
        for c in copies + more:
            c.start()
        hook()
        accs = [local_products(field[...], 0, selected(0)) for field in fields]
        rest = [local_products(field[...], 1, selected(1)) for field in others]
        out = border_products(accs, copies, 0, selected(0))
        rest = border_products(rest, more, 1, selected(1), 1)
        for c in copies + more:
            c.wait_send()
        return out, rest

    def first_half(fields, hook=None, border_hook=None):
        for f, value in enumerate(half(fields, 1, hook, border_hook)):
            odd_f[f] = value

    def second_half(fields, diagonal, hook=None, border_hook=None):
        odds = [odd_f.at[f] for f in range(len(fields))]
        values = half(odds, 0, hook, border_hook)
        return [diagonal * v[...] - d for v, d in zip(fields, values)]

    def stage_copies(blk, stage, place_of):
        copies = []
        for n, (device, place) in enumerate(peers(stage)):
            spot = my_place(stage) if place_of == "mine" else place
            copies.append(
                pltpu.make_async_remote_copy(
                    src_ref=row,
                    dst_ref=sums.at[stage, blk, spot],
                    send_sem=sum_send.at[n],
                    recv_sem=sum_recv.at[stage, blk, spot],
                    device_id=device,
                    device_id_type=mesh_id,
                )
            )
        return copies

    def stage_start(blk, stage, line):
        row[...] = line
        sums[stage, blk, my_place(stage)] = line
        for c in stage_copies(blk, stage, "mine"):
            c.start()

    def stage_end(blk, stage):
        for c in stage_copies(blk, stage, "theirs"):
            c.wait_send()
            c.wait_recv()
        return jnp.sum(sums[stage, blk], axis=0)

    lane = lax.broadcasted_iota(jnp.int32, (1, 128), 1)

    def line_of(pairs):
        rows = [jnp.sum(a * b, axis=0) for a, b in pairs]
        totals = jnp.sum(jnp.stack(rows), axis=1)
        totals = jnp.sum(totals, axis=1, keepdims=True)
        wide = (len(pairs), 128)
        own_lane = lax.broadcasted_iota(jnp.int32, wide, 0) == lax.broadcasted_iota(jnp.int32, wide, 1)
        return jnp.sum(jnp.where(own_lane, totals, 0.0), axis=0, keepdims=True)

    def local_dots():
        r, w, q = vec[0], vec[1], vec[2]
        m, v = prev[0], prev[1]
        return line_of(((r, r), (r, w), (w, w), (w, q), (r, m), (w, m), (w, v), (m, m), (m, v)))

    def moments():
        pairs = [(vec[(k + 1) // 2], vec[k // 2]) for k in range(7)]
        odd = odd_f[0]
        pairs += [(odd, odd)]
        pairs += [(vec[(k + 1) // 2], prev[k // 2]) for k in range(7)]
        pairs += [(prev[(k + 1) // 2], prev[k // 2]) for k in range(6)]
        return line_of(pairs)

    def spread(line, n):
        return jnp.broadcast_to(jnp.sum(jnp.where(lane == n, line, 0.0)), TILE)

    def times_each(a, b):
        out = [None] * (len(a) + len(b) - 1)
        for i, x in enumerate(a):
            for j, y in enumerate(b):
                out[i + j] = x * y if out[i + j] is None else out[i + j] + x * y
        return out

    def plus_each(a, b):
        return [x + y for x, y in zip(a, b)]

    def dots_from(line, both_steps, c):
        (_, _, u, f, h), (_, _, u1, f1, h1) = both_steps
        all_of = [spread(line, n) for n in range(21)]
        mu, nu, ka = all_of[:8], all_of[8:15], all_of[15:]
        mu[7] = mu[7] + (MASS - c) * mu[6]
        p5, q5 = [u, f], [h]
        p6, q6 = [u1 * u + h1, u1 * f + f1 * u, f1 * f], [u1 * h, f1 * h]

        def forms(p, q, p_, q_, powers):
            pp, qq = times_each(p, p_), times_each(q, q_)
            pq = plus_each(times_each(p, q_) + [jnp.zeros_like(u)] * 4, times_each(q, p_) + [jnp.zeros_like(u)] * 4)
            pq = pq[: max(len(p) + len(q_), len(q) + len(p_)) - 1]
            for k in powers:
                terms = [(a, m[n + k]) for s, m in ((pp, mu), (pq, nu), (qq, ka)) for n, a in enumerate(s)]
                total = terms[0][0] * terms[0][1]
                for a, m in terms[1:]:
                    total = total + a * m
                yield total

        rr, rw, ww, wq = forms(p6, q6, p6, q6, range(4))
        rm, wm, wv = forms(p6, q6, p5, q5, range(3))
        mm, mv = forms(p5, q5, p5, q5, range(2))
        return rr, rw, ww, wq, rm, wm, wv, mm, mv

    def coefficients(dots):
        rr, rw, ww, wq, rm, wm, wv, mm, mv = dots
        c = shift[...]
        step = rr / (rw + c * rr)
        scale = 1.0 / (1.0 - step * rr * kept[...])
        u, f, h = scale * (1.0 - step * c), -scale * step, 1.0 - scale
        rr1 = u * u * rr + f * f * ww + h * h * mm + 2.0 * (u * f * rw + u * h * rm + f * h * wm)
        rw1 = u * u * rw + f * f * wq + h * h * mv + 2.0 * (u * f * ww + u * h * wm + f * h * wv)
        mean1 = (rw1 + c * rr1) / rr1
        step1 = 1.0 / mean1
        scale1 = 1.0 / (1.0 - step1 * rr1 / (step * rr * scale))
        u1, f1, h1 = scale1 * (1.0 - step1 * c), -scale1 * step1, 1.0 - scale1
        kept[...] = 1.0 / (step1 * rr1 * scale1)
        return (step, scale, u, f, h), (step1, scale1, u1, f1, h1), mean1

    def early_update(line):
        (step, scale, u, f, h), (step1, scale1, u1, f1, h1), mean1 = coefficients(
            [spread(line, n) for n in range(DOTS)]
        )
        first = [u * vec[k] + f * vec[k + 1] + h * prev[k] for k in range(3)]
        second = [u1 * first[k] + f1 * first[k + 1] + h1 * vec[k] for k in range(2)]
        iterates(((step, scale, u, f, h), (step1, scale1, u1, f1, h1)), first[0])
        d = mean1 - shift[...]
        shift[...] = mean1
        half_first3 = u * vec[3] + h * prev[3]
        half_second2 = u1 * first[2] + h1 * vec[2]
        return d, f, f1, first, second, half_first3, half_second2

    def late_update(parts, fourth):
        d, f, f1, first, second, half_first3, half_second2 = parts
        first = first + [half_first3 + f * fourth]
        second = second + [half_second2 + f1 * first[3]]
        for stack, place in ((second, vec), (first, prev)):
            for k in range(len(stack)):
                place[k] = stack[0]
                stack = [b - d * a for a, b in zip(stack, stack[1:])]

    def iterates(both_steps, first):
        (step, scale, _, _, h), (step1, scale1, _, _, h1) = both_steps
        x, x0 = xs[0], xs[1]
        x1 = scale * (x + step * vec[0]) + h * x0
        xs[1] = x1
        xs[0] = scale1 * (x1 + step1 * first) + h1 * x

    def last_update(dots, r, w, q, m, v):
        (step, scale, u, f, h), (step1, scale1, u1, f1, h1), _ = coefficients(dots)
        c = shift[...]
        x, x0, ax, ax0 = xs[0], xs[1], images[0], images[1]
        r1 = u * r + f * w + h * m
        x1 = scale * (x + step * r) + h * x0
        x_out[...] = scale1 * (x1 + step1 * r1) + h1 * x
        ar = w + c * r
        ar1 = u * ar + f * (q + c * w) + h * (v + c * m)
        ax1 = scale * (ax + step * ar) + h * ax0
        t_out[...] = src_b[...] - (scale1 * (ax1 + step1 * ar1) + h1 * ax)

    loads[0].wait()
    vec[0] = src_b[...]
    prev[...] = jnp.zeros_like(prev)
    xs[...] = jnp.zeros_like(xs)
    kept[...] = jnp.zeros_like(kept)
    shift[...] = jnp.zeros_like(shift)

    def to_neighbour(src, field, n, side):
        return pltpu.make_async_remote_copy(
            src_ref=src,
            dst_ref=halo.at[1, field, n, side],
            send_sem=halo_send.at[1, field, n, side],
            recv_sem=halo_recv.at[1, field, n, side],
            device_id=at(AXES[n], 2 * side - 1),
            device_id_type=mesh_id,
        )

    def adjoint_product(links, mu, src):
        re = im = jnp.zeros((3, *TILE), jnp.float32)
        for i in range(3):
            lr = links[0, mu, pl.ds(3 * i, 3)].astype(jnp.float32)
            li = links[0, mu, pl.ds(9 + 3 * i, 3)].astype(jnp.float32)
            vr, vi = src[i][None], src[3 + i][None]
            re = re - lr * vr - li * vi
            im = im - lr * vi + li * vr
        return jnp.concatenate([re, im], axis=0)

    def opening_half():
        select = selected(1)
        forth = [to_neighbour(src_b, 0, n, 0) for n in range(3)]
        for c in forth:
            c.start()
        loads[1].wait()
        loads[2].wait()
        src = src_b[...]
        back = []
        for n in range(3):
            for kind in range(2):
                products[n, kind] = adjoint_product(kinds[1 - kind], n, src)
                back.append(to_neighbour(products.at[n, kind], kind, n, 1))
        for c in back:
            c.start()
        loads[3].wait()
        loads[4].wait()
        for p in (1, 0):
            for c in rim[p]:
                c.start()
        local_matrices(1)
        for mu, axis in enumerate(AXES):
            for kind in range(2):
                links = plain(kinds[kind], 1, mu)
                mats[1, 6 + 4 * mu + kind] = jnp.where(
                    inside(g, axis, kind, select), jnp.zeros_like(links), links
                )
        acc = local_products(src, 1, select)
        for axis, mu in (("gz", 1), ("gy", 2), ("ta", 0)):
            forth[mu].wait_recv()
            ahead = halo[1, 0, mu, 0]
            for kind in range(2):
                v = across(g, axis, kind, ahead, ahead, select)
                re, im = times(acc, 1, 6 + 4 * mu + kind, v)
                back[2 * mu + kind].wait_recv()
                made = turn(g, axis, kind, halo[1, kind, mu, 1], select)
                made = jnp.where(inside(g, axis, kind, select), made, 0.0)
                acc = (re + made[:3], im + made[3:])
        odd_f[0] = jnp.concatenate(acc, axis=0)
        for c in forth + back:
            c.wait_send()

    def link_sends_end():
        for copies in rim:
            for c in copies:
                c.wait_send()

    opening_half()
    (vec[1],) = second_half([src_b], MASS, lambda: local_matrices(0), lambda: border_matrices(0))
    link_sends_end()
    first_half([vec.at[1]], None, lambda: border_matrices(1))
    (vec[2],) = second_half([vec.at[1]], MASS)

    def block(blk, carry):
        diagonal = MASS - shift[...]
        first_half([vec.at[2]], lambda: stage_start(blk, 0, local_dots()))
        (vec[3],) = second_half(
            [vec.at[2]], diagonal, lambda: stage_start(blk, 1, stage_end(blk, 0))
        )
        first_half([vec.at[3]])
        parts = []
        (fourth,) = second_half(
            [vec.at[3]], diagonal, lambda: parts.extend(early_update(stage_end(blk, 1)))
        )
        late_update(parts, fourth)
        return carry

    lax.fori_loop(0, BLOCKS - 2, block, 0)

    blk, last = BLOCKS - 2, BLOCKS - 1
    c = shift[...]
    first_half([vec.at[2]], lambda: stage_start(blk, 0, local_dots()))
    (vec[3],) = second_half(
        [vec.at[2]], MASS - c, lambda: stage_start(blk, 1, stage_end(blk, 0))
    )
    known = []

    def steps_and_iterates():
        line = stage_end(blk, 1)
        a, b, _ = coefficients([spread(line, n) for n in range(DOTS)])
        known.extend((a, b))
        iterates(known, a[2] * vec[0] + a[3] * vec[1] + a[4] * prev[0])

    first_half([vec.at[3]], steps_and_iterates)
    both = [xs.at[0], xs.at[1]]
    (value,), odds = two_halves(
        [odd_f.at[0]], both, lambda: stage_start(last, 0, moments())
    )
    odd_f[1], odd_f[2] = odds
    fourth = (MASS - c) * vec[3] - value
    (_, _, u, f, h), (_, _, u1, f1, h1) = known
    powers = [vec[0], vec[1], vec[2], vec[3], fourth]
    before = [u * powers[k] + f * powers[k + 1] + h * prev[k] for k in range(4)]
    after = [u1 * before[k] + f1 * before[k + 1] + h1 * powers[k] for k in range(3)]
    values = half(
        [odd_f.at[1], odd_f.at[2]],
        0,
        lambda: stage_start(last, 1, stage_end(last, 0)),
        None,
        1,
    )
    for n in range(2):
        images[n] = MASS * xs[n] - values[n]
    last_update(dots_from(stage_end(last, 1), known, c), *after, *before[:2])


def per_device(source, fat_links, long_links):
    f32 = jnp.float32
    field = (6, *TILE)
    dma = pltpu.SemaphoreType.DMA
    fat = fat_links.reshape(2, 4, 18, *TILE)
    long = long_links.reshape(2, 4, 18, *TILE)
    vmem = pl.BlockSpec(memory_space=pltpu.VMEM)
    hbm = pl.BlockSpec(memory_space=pltpu.HBM)
    x, t = pl.pallas_call(
        kernel,
        out_shape=(pltpu.VMEM(field, f32), pltpu.VMEM(field, f32)),
        in_specs=[hbm] * 3,
        out_specs=(vmem, vmem),
        scratch_shapes=[
            pltpu.VMEM(fat.shape, fat.dtype),
            pltpu.VMEM(long.shape, long.dtype),
            pltpu.VMEM(field, f32),
            pltpu.VMEM((4, *field), f32),
            pltpu.VMEM((4, *field), f32),
            pltpu.VMEM((2, *field), f32),
            pltpu.VMEM((2, *field), f32),
            pltpu.VMEM((3, *field), f32),
            pltpu.VMEM((2, 16, 18, *TILE), f32),
            pltpu.VMEM((3, 2, *field), f32),
            pltpu.VMEM((2, 3, 3, 2, *field), f32),
            pltpu.VMEM((2, 3, 2, 18, *TILE), jnp.bfloat16),
            pltpu.VMEM((1, 128), f32),
            pltpu.VMEM((2, BLOCKS, MEMBERS, 1, 128), f32),
            pltpu.VMEM(TILE, f32),
            pltpu.VMEM(TILE, f32),
            dma((5,)),
            dma((2, 3, 3, 2)),
            dma((2, 3, 3, 2)),
            dma((2, 3, 2)),
            dma((2, 3, 2)),
            dma((MEMBERS - 1,)),
            dma((2, BLOCKS, MEMBERS)),
        ],
        compiler_params=pltpu.CompilerParams(
            collective_id=0, has_side_effects=True
        ),
    )(source.reshape(field), fat, long)
    return x.reshape(source.shape), t.reshape(source.shape)


def solution(mesh):
    field = P(None, None, "ta", "gz", "gy")
    links = P(None, None, None, None, None, "ta", "gz", "gy")
    return jax.shard_map(
        per_device,
        mesh=mesh,
        in_specs=(field, links, links),
        out_specs=(field, field),
        check_vma=False,
    )
```

```python
import jax
import jax.numpy as jnp
from jax import lax
from jax.experimental import pallas as pl
from jax.experimental.pallas import tpu as pltpu
from jax.sharding import PartitionSpec as P

NX = 32
BLOCKS = 4
MASS = 0.1
AXES = ("ta", "gz", "gy")
SIZES = {"ta": 4, "gz": 8, "gy": 8}
MEMBERS = 16
DOTS = 9
TILE = (8, 128)


def iota(axis):
    return lax.broadcasted_iota(jnp.int32, TILE, axis)


class Grid:
    def __init__(self):
        sub, lane = iota(0), iota(1)
        self.row, self.z = sub // 4, sub % 4
        self.lane, self.x = lane, lane % NX
        self.odd = (self.z + lane // NX + self.x) % 2 == 1


def roll(field, shift, axis):
    return pltpu.roll(field, shift % TILE[axis], axis + 1)


def turn(g, axis, kind, field, select):
    if axis == "ta":
        rolled = roll(field, 4, 0)
        return jnp.where(select, rolled, field) if kind == 0 else jnp.where(select, field, rolled)
    if axis == "gz":
        if kind == 0:
            return jnp.where(g.z < 3, roll(field, -1, 0), roll(field, 3, 0))
        return jnp.where(g.z > 0, roll(field, 1, 0), roll(field, -3, 0))
    return roll(field, -NX if kind == 0 else NX, 1)


def across(g, axis, kind, ahead, behind, select):
    if axis == "ta":
        rolled = roll(jnp.where(g.row == 0, ahead, behind), 4, 0)
        return jnp.where(select, rolled, behind) if kind == 0 else jnp.where(select, ahead, rolled)
    if axis == "gz":
        mixed = jnp.where(g.z == 0 if kind == 0 else g.z < 3, ahead, behind)
    else:
        mixed = jnp.where(g.lane < (NX if kind == 0 else 3 * NX), ahead, behind)
    return turn(g, axis, kind, mixed, select)


def inside(g, axis, kind, select):
    if axis == "ta":
        unselected = jnp.logical_not(select)
        first = g.row == 0
        return jnp.logical_or(unselected, first) if kind == 0 else jnp.logical_and(unselected, first)
    if axis == "gz":
        return g.z < 3 if kind == 0 else g.z == 0
    return g.lane < (3 * NX if kind == 0 else NX)


def along_x(g, by, field):
    if by > 0:
        return jnp.where(g.x < NX - by, roll(field, -by, 1), roll(field, NX - by, 1))
    return jnp.where(g.x >= -by, roll(field, -by, 1), roll(field, -by - NX, 1))


def kernel(
    b_hbm,
    fat_hbm,
    long_hbm,
    x_out,
    t_out,
    fat_ref,
    long_ref,
    src_b,
    vec,
    prev,
    xs,
    images,
    odd_f,
    mats,
    products,
    halo,
    rims,
    row,
    sums,
    kept,
    shift,
    load,
    halo_send,
    halo_recv,
    rim_send,
    rim_recv,
    sum_send,
    sum_recv,
):
    g = Grid()
    me = {a: lax.axis_index(a) for a in AXES}
    mesh_id = pl.DeviceIdType.MESH

    def at(axis, by):
        return {axis: lax.rem(me[axis] + (by % SIZES[axis]), SIZES[axis])}

    low, high = lax.rem(me["ta"], 2), me["ta"] // 2
    groups = (("gz", low, me["ta"] + 1 - 2 * low), ("gy", high, 3 - me["ta"]))

    def peers(stage):
        axis, bit, partner = groups[stage]
        for by in range(SIZES[axis]):
            there = lax.rem(me[axis] + by, SIZES[axis])
            if by:
                yield {axis: there}, 2 * there + bit
            yield {axis: there, "ta": partner}, 2 * there + 1 - bit

    def my_place(stage):
        axis, bit, _ = groups[stage]
        return 2 * me[axis] + bit

    barrier = pltpu.get_barrier_semaphore()
    for axis in AXES:
        for by in (-1, 1):
            pl.semaphore_signal(barrier, inc=1, device_id=at(axis, by), device_id_type=mesh_id)
    loads = [
        pltpu.make_async_copy(a, c, load.at[n])
        for n, (a, c) in enumerate(
            [(b_hbm, src_b)]
            + [(a.at[p], c.at[p]) for p in (0, 1) for a, c in ((fat_hbm, fat_ref), (long_hbm, long_ref))]
        )
    ]
    for c in loads:
        c.start()
    pl.semaphore_wait(barrier, 2 * len(AXES))

    def halo_copies(fields, slot, base=0):
        copies = []
        for n, axis in enumerate(AXES):
            for side, by in enumerate((-1, 1)):
                for f, src in enumerate(fields, base):
                    copies.append(
                        pltpu.make_async_remote_copy(
                            src_ref=src,
                            dst_ref=halo.at[slot, f, n, side],
                            send_sem=halo_send.at[slot, f, n, side],
                            recv_sem=halo_recv.at[slot, f, n, side],
                            device_id=at(axis, by),
                            device_id_type=mesh_id,
                        )
                    )
        return copies

    def rim_copies(p):
        copies = []
        for n, axis in enumerate(AXES):
            for kind, links in enumerate((fat_ref, long_ref)):
                copies.append(
                    pltpu.make_async_remote_copy(
                        src_ref=links.at[p, n],
                        dst_ref=rims.at[p, n, kind],
                        send_sem=rim_send.at[p, n, kind],
                        recv_sem=rim_recv.at[p, n, kind],
                        device_id=at(axis, 1),
                        device_id_type=mesh_id,
                    )
                )
        return copies

    def selected(dst):
        return g.odd if dst == 0 else jnp.logical_not(g.odd)

    rim = [rim_copies(0), rim_copies(1)]

    def plain(links, p, mu):
        columns = [links[p, mu, pl.ds(9 * part + j, 3, stride=3)] for part in (0, 1) for j in range(3)]
        return jnp.concatenate(columns, axis=0).astype(jnp.float32)

    def minus_adjoint(links):
        links = links.astype(jnp.float32)
        return jnp.concatenate([-links[:9], links[9:]], axis=0)

    kinds = (fat_ref, long_ref)
    X_HOPS = ((0, 1), (1, 3), (0, -1), (1, -3))

    def local_matrices(dst):
        select = selected(dst)
        for n, (kind, by) in enumerate(X_HOPS):
            if by > 0:
                mats[dst, n] = plain(kinds[kind], dst, 3)
            else:
                links = kinds[kind][1 - dst, 3].astype(jnp.float32)
                mats[dst, n] = minus_adjoint(along_x(g, by, links))
        for mu, axis in enumerate(AXES):
            for kind in range(2):
                links = kinds[1 - kind][1 - dst, mu].astype(jnp.float32)
                mats[dst, 4 + 4 * mu + kind] = jnp.where(
                    inside(g, axis, kind, select),
                    plain(kinds[kind], dst, mu),
                    minus_adjoint(turn(g, axis, kind, links, select)),
                )

    def border_matrices(dst):
        select = selected(dst)
        for mu, axis in enumerate(AXES):
            for kind in range(2):
                rim[1 - dst][2 * mu + 1 - kind].wait_recv()
                links = rims[1 - dst, mu, 1 - kind].astype(jnp.float32)
                mats[dst, 6 + 4 * mu + kind] = jnp.where(
                    inside(g, axis, kind, select),
                    minus_adjoint(turn(g, axis, kind, links, select)),
                    plain(kinds[kind], dst, mu),
                )

    def times(acc, dst, k, v):
        re, im = acc
        vr, vi = v[:3], v[3:]
        for j in range(3):
            mr, mi = mats[dst, k, pl.ds(3 * j, 3)], mats[dst, k, pl.ds(9 + 3 * j, 3)]
            re = re + mr * vr[j][None] - mi * vi[j][None]
            im = im + mr * vi[j][None] + mi * vr[j][None]
        return re, im

    def local_products(src, dst, select):
        acc = (jnp.zeros((3, *TILE), jnp.float32),) * 2
        for n, (_, by) in enumerate(X_HOPS):
            acc = times(acc, dst, n, along_x(g, by, src))
        for mu, axis in enumerate(AXES):
            for kind in range(2):
                acc = times(acc, dst, 4 + 4 * mu + kind, turn(g, axis, kind, src, select))
        return acc

    def border_products(accs, copies, dst, select, base=0):
        per_axis = 2 * len(accs)
        for axis, mu in (("gz", 1), ("gy", 2), ("ta", 0)):
            for c in copies[per_axis * mu : per_axis * (mu + 1)]:
                c.wait_recv()
            for f in range(len(accs)):
                ahead, behind = halo[dst, base + f, mu, 0], halo[dst, base + f, mu, 1]
                for kind in range(2):
                    v = across(g, axis, kind, ahead, behind, select)
                    accs[f] = times(accs[f], dst, 6 + 4 * mu + kind, v)
        return [jnp.concatenate(acc, axis=0) for acc in accs]

    def half(fields, dst, hook=None, border_hook=None, base=0):
        copies = halo_copies(fields, dst, base)
        for c in copies:
            c.start()
        if hook is not None:
            hook()
        select = selected(dst)
        accs = [local_products(field[...], dst, select) for field in fields]
        if border_hook is not None:
            border_hook()
        out = border_products(accs, copies, dst, select, base)
        for c in copies:
            c.wait_send()
        return out

    def two_halves(fields, others, hook):
        copies, more = halo_copies(fields, 0), halo_copies(others, 1, 1)
        hook()
        for c in copies + more:
            c.start()
        accs = [local_products(field[...], 0, selected(0)) for field in fields]
        rest = [local_products(field[...], 1, selected(1)) for field in others]
        out = border_products(accs, copies, 0, selected(0))
        rest = border_products(rest, more, 1, selected(1), 1)
        for c in copies + more:
            c.wait_send()
        return out, rest

    def first_half(fields, hook=None, border_hook=None):
        for f, value in enumerate(half(fields, 1, hook, border_hook)):
            odd_f[f] = value

    def second_half(fields, diagonal, hook=None, border_hook=None):
        odds = [odd_f.at[f] for f in range(len(fields))]
        values = half(odds, 0, hook, border_hook)
        return [diagonal * v[...] - d for v, d in zip(fields, values)]

    def stage_copies(blk, stage, place_of):
        copies = []
        for n, (device, place) in enumerate(peers(stage)):
            spot = my_place(stage) if place_of == "mine" else place
            copies.append(
                pltpu.make_async_remote_copy(
                    src_ref=row,
                    dst_ref=sums.at[stage, blk, spot],
                    send_sem=sum_send.at[n],
                    recv_sem=sum_recv.at[stage, blk, spot],
                    device_id=device,
                    device_id_type=mesh_id,
                )
            )
        return copies

    def stage_start(blk, stage, line):
        row[...] = line
        sums[stage, blk, my_place(stage)] = line
        for c in stage_copies(blk, stage, "mine"):
            c.start()

    def stage_end(blk, stage):
        for c in stage_copies(blk, stage, "theirs"):
            c.wait_send()
            c.wait_recv()
        return jnp.sum(sums[stage, blk], axis=0)

    lane = lax.broadcasted_iota(jnp.int32, (1, 128), 1)

    def line_of(pairs):
        rows = [jnp.sum(a * b, axis=0) for a, b in pairs]
        totals = jnp.sum(jnp.stack(rows), axis=1)
        totals = jnp.sum(totals, axis=1, keepdims=True)
        wide = (len(pairs), 128)
        own_lane = lax.broadcasted_iota(jnp.int32, wide, 0) == lax.broadcasted_iota(jnp.int32, wide, 1)
        return jnp.sum(jnp.where(own_lane, totals, 0.0), axis=0, keepdims=True)

    def local_dots():
        r, w, q = vec[0], vec[1], vec[2]
        m, v = prev[0], prev[1]
        return line_of(((r, r), (r, w), (w, w), (w, q), (r, m), (w, m), (w, v), (m, m), (m, v)))

    def moments():
        pairs = [(vec[(k + 1) // 2], vec[k // 2]) for k in range(7)]
        pairs += [(vec[(k + 1) // 2], prev[k // 2]) for k in range(7)]
        pairs += [(prev[(k + 1) // 2], prev[k // 2]) for k in range(6)]
        return line_of(pairs)

    def spread(line, n):
        return jnp.broadcast_to(jnp.sum(jnp.where(lane == n, line, 0.0)), TILE)

    def times_each(a, b):
        out = [None] * (len(a) + len(b) - 1)
        for i, x in enumerate(a):
            for j, y in enumerate(b):
                out[i + j] = x * y if out[i + j] is None else out[i + j] + x * y
        return out

    def plus_each(a, b):
        return [x + y for x, y in zip(a, b)]

    def dots_from(line, both_steps, c):
        (_, _, u, f, h), (_, _, u1, f1, h1) = both_steps
        all_of = [spread(line, n) for n in range(21)]
        mu, nu, ka = all_of[:7] + all_of[20:], all_of[7:14], all_of[14:20]
        mu[7] = mu[7] + (MASS - c) * mu[6]
        p5, q5 = [u, f], [h]
        p6, q6 = [u1 * u + h1, u1 * f + f1 * u, f1 * f], [u1 * h, f1 * h]

        def forms(p, q, p_, q_, powers):
            pp, qq = times_each(p, p_), times_each(q, q_)
            pq = plus_each(times_each(p, q_) + [jnp.zeros_like(u)] * 4, times_each(q, p_) + [jnp.zeros_like(u)] * 4)
            pq = pq[: max(len(p) + len(q_), len(q) + len(p_)) - 1]
            for k in powers:
                terms = [(a, m[n + k]) for s, m in ((pp, mu), (pq, nu), (qq, ka)) for n, a in enumerate(s)]
                total = terms[0][0] * terms[0][1]
                for a, m in terms[1:]:
                    total = total + a * m
                yield total

        rr, rw, ww, wq = forms(p6, q6, p6, q6, range(4))
        rm, wm, wv = forms(p6, q6, p5, q5, range(3))
        mm, mv = forms(p5, q5, p5, q5, range(2))
        return rr, rw, ww, wq, rm, wm, wv, mm, mv

    def coefficients(dots):
        rr, rw, ww, wq, rm, wm, wv, mm, mv = dots
        c = shift[...]
        step = rr / (rw + c * rr)
        scale = 1.0 / (1.0 - step * rr * kept[...])
        u, f, h = scale * (1.0 - step * c), -scale * step, 1.0 - scale
        rr1 = u * u * rr + f * f * ww + h * h * mm + 2.0 * (u * f * rw + u * h * rm + f * h * wm)
        rw1 = u * u * rw + f * f * wq + h * h * mv + 2.0 * (u * f * ww + u * h * wm + f * h * wv)
        mean1 = (rw1 + c * rr1) / rr1
        step1 = 1.0 / mean1
        scale1 = 1.0 / (1.0 - step1 * rr1 / (step * rr * scale))
        u1, f1, h1 = scale1 * (1.0 - step1 * c), -scale1 * step1, 1.0 - scale1
        kept[...] = 1.0 / (step1 * rr1 * scale1)
        return (step, scale, u, f, h), (step1, scale1, u1, f1, h1), mean1

    def early_update(line):
        (step, scale, u, f, h), (step1, scale1, u1, f1, h1), mean1 = coefficients(
            [spread(line, n) for n in range(DOTS)]
        )
        first = [u * vec[k] + f * vec[k + 1] + h * prev[k] for k in range(3)]
        second = [u1 * first[k] + f1 * first[k + 1] + h1 * vec[k] for k in range(2)]
        iterates(((step, scale, u, f, h), (step1, scale1, u1, f1, h1)), first[0])
        d = mean1 - shift[...]
        shift[...] = mean1
        half_first3 = u * vec[3] + h * prev[3]
        half_second2 = u1 * first[2] + h1 * vec[2]
        return d, f, f1, first, second, half_first3, half_second2

    def late_update(parts, fourth):
        d, f, f1, first, second, half_first3, half_second2 = parts
        first = first + [half_first3 + f * fourth]
        second = second + [half_second2 + f1 * first[3]]
        for stack, place in ((second, vec), (first, prev)):
            for k in range(len(stack)):
                place[k] = stack[0]
                stack = [b - d * a for a, b in zip(stack, stack[1:])]

    def iterates(both_steps, first):
        (step, scale, _, _, h), (step1, scale1, _, _, h1) = both_steps
        x, x0 = xs[0], xs[1]
        x1 = scale * (x + step * vec[0]) + h * x0
        xs[1] = x1
        xs[0] = scale1 * (x1 + step1 * first) + h1 * x

    def last_update(dots, r, w, q, m, v):
        (step, scale, u, f, h), (step1, scale1, u1, f1, h1), _ = coefficients(dots)
        c = shift[...]
        x, x0, ax, ax0 = xs[0], xs[1], images[0], images[1]
        r1 = u * r + f * w + h * m
        x1 = scale * (x + step * r) + h * x0
        x_out[...] = scale1 * (x1 + step1 * r1) + h1 * x
        ar = w + c * r
        ar1 = u * ar + f * (q + c * w) + h * (v + c * m)
        ax1 = scale * (ax + step * ar) + h * ax0
        t_out[...] = src_b[...] - (scale1 * (ax1 + step1 * ar1) + h1 * ax)

    loads[0].wait()
    vec[0] = src_b[...]
    prev[...] = jnp.zeros_like(prev)
    xs[...] = jnp.zeros_like(xs)
    kept[...] = jnp.zeros_like(kept)
    shift[...] = jnp.zeros_like(shift)

    def to_neighbour(src, field, n, side):
        return pltpu.make_async_remote_copy(
            src_ref=src,
            dst_ref=halo.at[1, field, n, side],
            send_sem=halo_send.at[1, field, n, side],
            recv_sem=halo_recv.at[1, field, n, side],
            device_id=at(AXES[n], 2 * side - 1),
            device_id_type=mesh_id,
        )

    def adjoint_product(links, mu, src):
        re = im = jnp.zeros((3, *TILE), jnp.float32)
        for i in range(3):
            lr = links[0, mu, pl.ds(3 * i, 3)].astype(jnp.float32)
            li = links[0, mu, pl.ds(9 + 3 * i, 3)].astype(jnp.float32)
            vr, vi = src[i][None], src[3 + i][None]
            re = re - lr * vr - li * vi
            im = im - lr * vi + li * vr
        return jnp.concatenate([re, im], axis=0)

    def opening_half():
        select = selected(1)
        forth = [to_neighbour(src_b, 0, n, 0) for n in range(3)]
        for c in forth:
            c.start()
        loads[1].wait()
        loads[2].wait()
        src = src_b[...]
        back = []
        for n in range(3):
            for kind in range(2):
                products[n, kind] = adjoint_product(kinds[1 - kind], n, src)
                back.append(to_neighbour(products.at[n, kind], kind, n, 1))
        for c in back:
            c.start()
        loads[3].wait()
        loads[4].wait()
        for p in (1, 0):
            for c in rim[p]:
                c.start()
        local_matrices(1)
        for mu, axis in enumerate(AXES):
            for kind in range(2):
                links = plain(kinds[kind], 1, mu)
                mats[1, 6 + 4 * mu + kind] = jnp.where(
                    inside(g, axis, kind, select), jnp.zeros_like(links), links
                )
        acc = local_products(src, 1, select)
        for axis, mu in (("gz", 1), ("gy", 2), ("ta", 0)):
            forth[mu].wait_recv()
            ahead = halo[1, 0, mu, 0]
            for kind in range(2):
                v = across(g, axis, kind, ahead, ahead, select)
                re, im = times(acc, 1, 6 + 4 * mu + kind, v)
                back[2 * mu + kind].wait_recv()
                made = turn(g, axis, kind, halo[1, kind, mu, 1], select)
                made = jnp.where(inside(g, axis, kind, select), made, 0.0)
                acc = (re + made[:3], im + made[3:])
        odd_f[0] = jnp.concatenate(acc, axis=0)
        for c in forth + back:
            c.wait_send()

    def link_sends_end():
        for copies in rim:
            for c in copies:
                c.wait_send()

    opening_half()
    (vec[1],) = second_half([src_b], MASS, lambda: local_matrices(0), lambda: border_matrices(0))
    link_sends_end()
    first_half([vec.at[1]], None, lambda: border_matrices(1))
    (vec[2],) = second_half([vec.at[1]], MASS)

    def block(blk, carry):
        diagonal = MASS - shift[...]
        first_half([vec.at[2]], lambda: stage_start(blk, 0, local_dots()))
        (vec[3],) = second_half(
            [vec.at[2]], diagonal, lambda: stage_start(blk, 1, stage_end(blk, 0))
        )
        first_half([vec.at[3]])
        parts = []
        (fourth,) = second_half(
            [vec.at[3]], diagonal, lambda: parts.extend(early_update(stage_end(blk, 1)))
        )
        late_update(parts, fourth)
        return carry

    lax.fori_loop(0, BLOCKS - 2, block, 0)

    blk, last = BLOCKS - 2, BLOCKS - 1
    c = shift[...]
    first_half([vec.at[2]], lambda: stage_start(blk, 0, local_dots()))
    (vec[3],) = second_half(
        [vec.at[2]], MASS - c, lambda: stage_start(blk, 1, stage_end(blk, 0))
    )
    known = []

    def steps_and_iterates():
        line = stage_end(blk, 1)
        a, b, _ = coefficients([spread(line, n) for n in range(DOTS)])
        iterates((a, b), a[2] * vec[0] + a[3] * vec[1] + a[4] * prev[0])
        known.extend((a, b, moments()))

    first_half([vec.at[3]], steps_and_iterates)
    ready = known.pop()
    both = [xs.at[0], xs.at[1]]

    def last_moment():
        odd = odd_f[0]
        stage_start(last, 0, ready + jnp.where(lane == 20, jnp.sum(odd * odd), 0.0))

    (value,), odds = two_halves([odd_f.at[0]], both, last_moment)
    odd_f[1], odd_f[2] = odds
    fourth = (MASS - c) * vec[3] - value
    (_, _, u, f, h), (_, _, u1, f1, h1) = known
    powers = [vec[0], vec[1], vec[2], vec[3], fourth]
    before = [u * powers[k] + f * powers[k + 1] + h * prev[k] for k in range(4)]
    after = [u1 * before[k] + f1 * before[k + 1] + h1 * powers[k] for k in range(3)]
    stage_start(last, 1, stage_end(last, 0))
    values = half([odd_f.at[1], odd_f.at[2]], 0, base=1)
    for n in range(2):
        images[n] = MASS * xs[n] - values[n]
    last_update(dots_from(stage_end(last, 1), known, c), *after, *before[:2])


def per_device(source, fat_links, long_links):
    f32 = jnp.float32
    field = (6, *TILE)
    dma = pltpu.SemaphoreType.DMA
    fat = fat_links.reshape(2, 4, 18, *TILE)
    long = long_links.reshape(2, 4, 18, *TILE)
    vmem = pl.BlockSpec(memory_space=pltpu.VMEM)
    hbm = pl.BlockSpec(memory_space=pltpu.HBM)
    x, t = pl.pallas_call(
        kernel,
        out_shape=(pltpu.VMEM(field, f32), pltpu.VMEM(field, f32)),
        in_specs=[hbm] * 3,
        out_specs=(vmem, vmem),
        scratch_shapes=[
            pltpu.VMEM(fat.shape, fat.dtype),
            pltpu.VMEM(long.shape, long.dtype),
            pltpu.VMEM(field, f32),
            pltpu.VMEM((4, *field), f32),
            pltpu.VMEM((4, *field), f32),
            pltpu.VMEM((2, *field), f32),
            pltpu.VMEM((2, *field), f32),
            pltpu.VMEM((3, *field), f32),
            pltpu.VMEM((2, 16, 18, *TILE), f32),
            pltpu.VMEM((3, 2, *field), f32),
            pltpu.VMEM((2, 3, 3, 2, *field), f32),
            pltpu.VMEM((2, 3, 2, 18, *TILE), jnp.bfloat16),
            pltpu.VMEM((1, 128), f32),
            pltpu.VMEM((2, BLOCKS, MEMBERS, 1, 128), f32),
            pltpu.VMEM(TILE, f32),
            pltpu.VMEM(TILE, f32),
            dma((5,)),
            dma((2, 3, 3, 2)),
            dma((2, 3, 3, 2)),
            dma((2, 3, 2)),
            dma((2, 3, 2)),
            dma((MEMBERS - 1,)),
            dma((2, BLOCKS, MEMBERS)),
        ],
        compiler_params=pltpu.CompilerParams(
            collective_id=0, has_side_effects=True
        ),
    )(source.reshape(field), fat, long)
    return x.reshape(source.shape), t.reshape(source.shape)


def solution(mesh):
    field = P(None, None, "ta", "gz", "gy")
    links = P(None, None, None, None, None, "ta", "gz", "gy")
    return jax.shard_map(
        per_device,
        mesh=mesh,
        in_specs=(field, links, links),
        out_specs=(field, field),
        check_vma=False,
    )
```

```python
import jax
import jax.numpy as jnp
from jax import lax
from jax.experimental import pallas as pl
from jax.experimental.pallas import tpu as pltpu
from jax.sharding import PartitionSpec as P

NX = 32
BLOCKS = 4
MASS = 0.1
AXES = ("ta", "gz", "gy")
SIZES = {"ta": 4, "gz": 8, "gy": 8}
MEMBERS = 16
DOTS = 9
TILE = (8, 128)


def iota(axis):
    return lax.broadcasted_iota(jnp.int32, TILE, axis)


class Grid:
    def __init__(self):
        sub, lane = iota(0), iota(1)
        self.row, self.z = sub // 4, sub % 4
        self.lane, self.x = lane, lane % NX
        self.odd = (self.z + lane // NX + self.x) % 2 == 1


def roll(field, shift, axis):
    return pltpu.roll(field, shift % TILE[axis], axis + 1)


def turn(g, axis, kind, field, select):
    if axis == "ta":
        rolled = roll(field, 4, 0)
        return jnp.where(select, rolled, field) if kind == 0 else jnp.where(select, field, rolled)
    if axis == "gz":
        if kind == 0:
            return jnp.where(g.z < 3, roll(field, -1, 0), roll(field, 3, 0))
        return jnp.where(g.z > 0, roll(field, 1, 0), roll(field, -3, 0))
    return roll(field, -NX if kind == 0 else NX, 1)


def across(g, axis, kind, ahead, behind, select):
    if axis == "ta":
        rolled = roll(jnp.where(g.row == 0, ahead, behind), 4, 0)
        return jnp.where(select, rolled, behind) if kind == 0 else jnp.where(select, ahead, rolled)
    if axis == "gz":
        mixed = jnp.where(g.z == 0 if kind == 0 else g.z < 3, ahead, behind)
    else:
        mixed = jnp.where(g.lane < (NX if kind == 0 else 3 * NX), ahead, behind)
    return turn(g, axis, kind, mixed, select)


def inside(g, axis, kind, select):
    if axis == "ta":
        unselected = jnp.logical_not(select)
        first = g.row == 0
        return jnp.logical_or(unselected, first) if kind == 0 else jnp.logical_and(unselected, first)
    if axis == "gz":
        return g.z < 3 if kind == 0 else g.z == 0
    return g.lane < (3 * NX if kind == 0 else NX)


def along_x(g, by, field):
    if by > 0:
        return jnp.where(g.x < NX - by, roll(field, -by, 1), roll(field, NX - by, 1))
    return jnp.where(g.x >= -by, roll(field, -by, 1), roll(field, -by - NX, 1))


def kernel(
    b_hbm,
    fat_hbm,
    long_hbm,
    x_out,
    t_out,
    fat_ref,
    long_ref,
    src_b,
    vec,
    prev,
    xs,
    images,
    odd_f,
    mats,
    products,
    halo,
    rims,
    row,
    sums,
    kept,
    shift,
    load,
    halo_send,
    halo_recv,
    rim_send,
    rim_recv,
    sum_send,
    sum_recv,
):
    g = Grid()
    me = {a: lax.axis_index(a) for a in AXES}
    mesh_id = pl.DeviceIdType.MESH

    def at(axis, by):
        return {axis: lax.rem(me[axis] + (by % SIZES[axis]), SIZES[axis])}

    low, high = lax.rem(me["ta"], 2), me["ta"] // 2
    groups = (("gz", low, me["ta"] + 1 - 2 * low), ("gy", high, 3 - me["ta"]))

    def peers(stage):
        axis, bit, partner = groups[stage]
        for by in range(SIZES[axis]):
            there = lax.rem(me[axis] + by, SIZES[axis])
            if by:
                yield {axis: there}, 2 * there + bit
            yield {axis: there, "ta": partner}, 2 * there + 1 - bit

    def my_place(stage):
        axis, bit, _ = groups[stage]
        return 2 * me[axis] + bit

    barrier = pltpu.get_barrier_semaphore()
    for axis in AXES:
        for by in (-1, 1):
            pl.semaphore_signal(barrier, inc=1, device_id=at(axis, by), device_id_type=mesh_id)
    loads = [
        pltpu.make_async_copy(a, c, load.at[n])
        for n, (a, c) in enumerate(
            [(b_hbm, src_b)]
            + [(a.at[p], c.at[p]) for p in (0, 1) for a, c in ((fat_hbm, fat_ref), (long_hbm, long_ref))]
        )
    ]
    for c in loads:
        c.start()
    pl.semaphore_wait(barrier, 2 * len(AXES))

    def halo_copies(fields, slot, base=0):
        copies = []
        for n, axis in enumerate(AXES):
            for side, by in enumerate((-1, 1)):
                for f, src in enumerate(fields, base):
                    copies.append(
                        pltpu.make_async_remote_copy(
                            src_ref=src,
                            dst_ref=halo.at[slot, f, n, side],
                            send_sem=halo_send.at[slot, f, n, side],
                            recv_sem=halo_recv.at[slot, f, n, side],
                            device_id=at(axis, by),
                            device_id_type=mesh_id,
                        )
                    )
        return copies

    def rim_copies(p):
        copies = []
        for n, axis in enumerate(AXES):
            for kind, links in enumerate((fat_ref, long_ref)):
                copies.append(
                    pltpu.make_async_remote_copy(
                        src_ref=links.at[p, n],
                        dst_ref=rims.at[p, n, kind],
                        send_sem=rim_send.at[p, n, kind],
                        recv_sem=rim_recv.at[p, n, kind],
                        device_id=at(axis, 1),
                        device_id_type=mesh_id,
                    )
                )
        return copies

    def selected(dst):
        return g.odd if dst == 0 else jnp.logical_not(g.odd)

    rim = [rim_copies(0), rim_copies(1)]

    def plain(links, p, mu):
        columns = [links[p, mu, pl.ds(9 * part + j, 3, stride=3)] for part in (0, 1) for j in range(3)]
        return jnp.concatenate(columns, axis=0).astype(jnp.float32)

    def minus_adjoint(links):
        links = links.astype(jnp.float32)
        return jnp.concatenate([-links[:9], links[9:]], axis=0)

    kinds = (fat_ref, long_ref)
    X_HOPS = ((0, 1), (1, 3), (0, -1), (1, -3))

    def local_matrices(dst):
        select = selected(dst)
        for n, (kind, by) in enumerate(X_HOPS):
            if by > 0:
                mats[dst, n] = plain(kinds[kind], dst, 3)
            else:
                links = kinds[kind][1 - dst, 3].astype(jnp.float32)
                mats[dst, n] = minus_adjoint(along_x(g, by, links))
        for mu, axis in enumerate(AXES):
            for kind in range(2):
                links = kinds[1 - kind][1 - dst, mu].astype(jnp.float32)
                mats[dst, 4 + 4 * mu + kind] = jnp.where(
                    inside(g, axis, kind, select),
                    plain(kinds[kind], dst, mu),
                    minus_adjoint(turn(g, axis, kind, links, select)),
                )

    def border_matrices(dst):
        select = selected(dst)
        for mu, axis in enumerate(AXES):
            for kind in range(2):
                rim[1 - dst][2 * mu + 1 - kind].wait_recv()
                links = rims[1 - dst, mu, 1 - kind].astype(jnp.float32)
                mats[dst, 6 + 4 * mu + kind] = jnp.where(
                    inside(g, axis, kind, select),
                    minus_adjoint(turn(g, axis, kind, links, select)),
                    plain(kinds[kind], dst, mu),
                )

    def times(acc, dst, k, v):
        re, im = acc
        vr, vi = v[:3], v[3:]
        for j in range(3):
            mr, mi = mats[dst, k, pl.ds(3 * j, 3)], mats[dst, k, pl.ds(9 + 3 * j, 3)]
            re = re + mr * vr[j][None] - mi * vi[j][None]
            im = im + mr * vi[j][None] + mi * vr[j][None]
        return re, im

    def local_products(src, dst, select):
        acc = (jnp.zeros((3, *TILE), jnp.float32),) * 2
        for n, (_, by) in enumerate(X_HOPS):
            acc = times(acc, dst, n, along_x(g, by, src))
        for mu, axis in enumerate(AXES):
            for kind in range(2):
                acc = times(acc, dst, 4 + 4 * mu + kind, turn(g, axis, kind, src, select))
        return acc

    def border_products(accs, copies, dst, select, base=0):
        per_axis = 2 * len(accs)
        for axis, mu in (("gz", 1), ("gy", 2), ("ta", 0)):
            for c in copies[per_axis * mu : per_axis * (mu + 1)]:
                c.wait_recv()
            for f in range(len(accs)):
                ahead, behind = halo[dst, base + f, mu, 0], halo[dst, base + f, mu, 1]
                for kind in range(2):
                    v = across(g, axis, kind, ahead, behind, select)
                    accs[f] = times(accs[f], dst, 6 + 4 * mu + kind, v)
        return [jnp.concatenate(acc, axis=0) for acc in accs]

    def half(fields, dst, hook=None, border_hook=None, base=0):
        copies = halo_copies(fields, dst, base)
        for c in copies:
            c.start()
        if hook is not None:
            hook()
        select = selected(dst)
        accs = [local_products(field[...], dst, select) for field in fields]
        if border_hook is not None:
            border_hook()
        out = border_products(accs, copies, dst, select, base)
        for c in copies:
            c.wait_send()
        return out

    def two_halves(fields, others, hook):
        copies, more = halo_copies(fields, 0), halo_copies(others, 1, 1)
        hook()
        for c in copies + more:
            c.start()
        accs = [local_products(field[...], 0, selected(0)) for field in fields]
        rest = [local_products(field[...], 1, selected(1)) for field in others]
        out = border_products(accs, copies, 0, selected(0))
        rest = border_products(rest, more, 1, selected(1), 1)
        for c in copies + more:
            c.wait_send()
        return out, rest

    def first_half(fields, hook=None, border_hook=None):
        for f, value in enumerate(half(fields, 1, hook, border_hook)):
            odd_f[f] = value

    def second_half(fields, diagonal, hook=None, border_hook=None):
        odds = [odd_f.at[f] for f in range(len(fields))]
        values = half(odds, 0, hook, border_hook)
        return [diagonal * v[...] - d for v, d in zip(fields, values)]

    def stage_copies(blk, stage, place_of):
        copies = []
        for n, (device, place) in enumerate(peers(stage)):
            spot = my_place(stage) if place_of == "mine" else place
            copies.append(
                pltpu.make_async_remote_copy(
                    src_ref=row,
                    dst_ref=sums.at[stage, blk, spot],
                    send_sem=sum_send.at[n],
                    recv_sem=sum_recv.at[stage, blk, spot],
                    device_id=device,
                    device_id_type=mesh_id,
                )
            )
        return copies

    def stage_start(blk, stage, line):
        row[...] = line
        sums[stage, blk, my_place(stage)] = line
        for c in stage_copies(blk, stage, "mine"):
            c.start()

    def stage_end(blk, stage):
        for c in stage_copies(blk, stage, "theirs"):
            c.wait_send()
            c.wait_recv()
        return jnp.sum(sums[stage, blk], axis=0)

    lane = lax.broadcasted_iota(jnp.int32, (1, 128), 1)

    def line_of(pairs):
        rows = [jnp.sum(a * b, axis=0) for a, b in pairs]
        totals = jnp.sum(jnp.stack(rows), axis=1)
        totals = jnp.sum(totals, axis=1, keepdims=True)
        wide = (len(pairs), 128)
        own_lane = lax.broadcasted_iota(jnp.int32, wide, 0) == lax.broadcasted_iota(jnp.int32, wide, 1)
        return jnp.sum(jnp.where(own_lane, totals, 0.0), axis=0, keepdims=True)

    def local_dots():
        r, w, q = vec[0], vec[1], vec[2]
        m, v = prev[0], prev[1]
        return line_of(((r, r), (r, w), (w, w), (w, q), (r, m), (w, m), (w, v), (m, m), (m, v)))

    def moments():
        pairs = [(vec[(k + 1) // 2], vec[k // 2]) for k in range(7)]
        pairs += [(vec[(k + 1) // 2], prev[k // 2]) for k in range(7)]
        pairs += [(prev[(k + 1) // 2], prev[k // 2]) for k in range(6)]
        return line_of(pairs)

    def spread(line, n):
        return jnp.broadcast_to(line[:, n : n + 1], TILE)

    def times_each(a, b):
        out = [None] * (len(a) + len(b) - 1)
        for i, x in enumerate(a):
            for j, y in enumerate(b):
                out[i + j] = x * y if out[i + j] is None else out[i + j] + x * y
        return out

    def plus_each(a, b):
        return [x + y for x, y in zip(a, b)]

    def dots_from(line, both_steps, c):
        (_, _, u, f, h), (_, _, u1, f1, h1) = both_steps
        all_of = [spread(line, n) for n in range(21)]
        mu, nu, ka = all_of[:7] + all_of[20:], all_of[7:14], all_of[14:20]
        mu[7] = mu[7] + (MASS - c) * mu[6]
        p5, q5 = [u, f], [h]
        p6, q6 = [u1 * u + h1, u1 * f + f1 * u, f1 * f], [u1 * h, f1 * h]

        def forms(p, q, p_, q_, powers):
            pp, qq = times_each(p, p_), times_each(q, q_)
            pq = plus_each(times_each(p, q_) + [jnp.zeros_like(u)] * 4, times_each(q, p_) + [jnp.zeros_like(u)] * 4)
            pq = pq[: max(len(p) + len(q_), len(q) + len(p_)) - 1]
            for k in powers:
                terms = [(a, m[n + k]) for s, m in ((pp, mu), (pq, nu), (qq, ka)) for n, a in enumerate(s)]
                total = terms[0][0] * terms[0][1]
                for a, m in terms[1:]:
                    total = total + a * m
                yield total

        rr, rw, ww, wq = forms(p6, q6, p6, q6, range(4))
        rm, wm, wv = forms(p6, q6, p5, q5, range(3))
        mm, mv = forms(p5, q5, p5, q5, range(2))
        return rr, rw, ww, wq, rm, wm, wv, mm, mv

    def coefficients(dots):
        rr, rw, ww, wq, rm, wm, wv, mm, mv = dots
        c = shift[...]
        step = rr / (rw + c * rr)
        scale = 1.0 / (1.0 - step * rr * kept[...])
        u, f, h = scale * (1.0 - step * c), -scale * step, 1.0 - scale
        rr1 = u * u * rr + f * f * ww + h * h * mm + 2.0 * (u * f * rw + u * h * rm + f * h * wm)
        rw1 = u * u * rw + f * f * wq + h * h * mv + 2.0 * (u * f * ww + u * h * wm + f * h * wv)
        mean1 = (rw1 + c * rr1) / rr1
        step1 = 1.0 / mean1
        scale1 = 1.0 / (1.0 - step1 * rr1 / (step * rr * scale))
        u1, f1, h1 = scale1 * (1.0 - step1 * c), -scale1 * step1, 1.0 - scale1
        kept[...] = 1.0 / (step1 * rr1 * scale1)
        return (step, scale, u, f, h), (step1, scale1, u1, f1, h1), mean1

    def early_update(line):
        (step, scale, u, f, h), (step1, scale1, u1, f1, h1), mean1 = coefficients(
            [spread(line, n) for n in range(DOTS)]
        )
        first = [u * vec[k] + f * vec[k + 1] + h * prev[k] for k in range(3)]
        second = [u1 * first[k] + f1 * first[k + 1] + h1 * vec[k] for k in range(2)]
        iterates(((step, scale, u, f, h), (step1, scale1, u1, f1, h1)), first[0])
        d = mean1 - shift[...]
        shift[...] = mean1
        half_first3 = u * vec[3] + h * prev[3]
        half_second2 = u1 * first[2] + h1 * vec[2]
        return d, f, f1, first, second, half_first3, half_second2

    def late_update(parts, fourth):
        d, f, f1, first, second, half_first3, half_second2 = parts
        first = first + [half_first3 + f * fourth]
        second = second + [half_second2 + f1 * first[3]]
        for stack, place in ((second, vec), (first, prev)):
            for k in range(len(stack)):
                place[k] = stack[0]
                stack = [b - d * a for a, b in zip(stack, stack[1:])]

    def iterates(both_steps, first):
        (step, scale, _, _, h), (step1, scale1, _, _, h1) = both_steps
        x, x0 = xs[0], xs[1]
        x1 = scale * (x + step * vec[0]) + h * x0
        xs[1] = x1
        xs[0] = scale1 * (x1 + step1 * first) + h1 * x

    def last_update(dots, r, w, q, m, v):
        (step, scale, u, f, h), (step1, scale1, u1, f1, h1), _ = coefficients(dots)
        c = shift[...]
        x, x0, ax, ax0 = xs[0], xs[1], images[0], images[1]
        r1 = u * r + f * w + h * m
        x1 = scale * (x + step * r) + h * x0
        x_out[...] = scale1 * (x1 + step1 * r1) + h1 * x
        ar = w + c * r
        ar1 = u * ar + f * (q + c * w) + h * (v + c * m)
        ax1 = scale * (ax + step * ar) + h * ax0
        t_out[...] = src_b[...] - (scale1 * (ax1 + step1 * ar1) + h1 * ax)

    loads[0].wait()
    vec[0] = src_b[...]
    prev[...] = jnp.zeros_like(prev)
    xs[...] = jnp.zeros_like(xs)
    kept[...] = jnp.zeros_like(kept)
    shift[...] = jnp.zeros_like(shift)

    def to_neighbour(src, field, n, side):
        return pltpu.make_async_remote_copy(
            src_ref=src,
            dst_ref=halo.at[1, field, n, side],
            send_sem=halo_send.at[1, field, n, side],
            recv_sem=halo_recv.at[1, field, n, side],
            device_id=at(AXES[n], 2 * side - 1),
            device_id_type=mesh_id,
        )

    def adjoint_product(links, mu, src):
        re = im = jnp.zeros((3, *TILE), jnp.float32)
        for i in range(3):
            lr = links[0, mu, pl.ds(3 * i, 3)].astype(jnp.float32)
            li = links[0, mu, pl.ds(9 + 3 * i, 3)].astype(jnp.float32)
            vr, vi = src[i][None], src[3 + i][None]
            re = re - lr * vr - li * vi
            im = im - lr * vi + li * vr
        return jnp.concatenate([re, im], axis=0)

    def opening_half():
        select = selected(1)
        forth = [to_neighbour(src_b, 0, n, 0) for n in range(3)]
        for c in forth:
            c.start()
        loads[1].wait()
        loads[2].wait()
        src = src_b[...]
        back = []
        for n in range(3):
            for kind in range(2):
                products[n, kind] = adjoint_product(kinds[1 - kind], n, src)
                back.append(to_neighbour(products.at[n, kind], kind, n, 1))
        for c in back:
            c.start()
        loads[3].wait()
        loads[4].wait()
        for p in (1, 0):
            for c in rim[p]:
                c.start()
        local_matrices(1)
        for mu, axis in enumerate(AXES):
            for kind in range(2):
                links = plain(kinds[kind], 1, mu)
                mats[1, 6 + 4 * mu + kind] = jnp.where(
                    inside(g, axis, kind, select), jnp.zeros_like(links), links
                )
        acc = local_products(src, 1, select)
        for axis, mu in (("gz", 1), ("gy", 2), ("ta", 0)):
            forth[mu].wait_recv()
            ahead = halo[1, 0, mu, 0]
            for kind in range(2):
                v = across(g, axis, kind, ahead, ahead, select)
                re, im = times(acc, 1, 6 + 4 * mu + kind, v)
                back[2 * mu + kind].wait_recv()
                made = turn(g, axis, kind, halo[1, kind, mu, 1], select)
                made = jnp.where(inside(g, axis, kind, select), made, 0.0)
                acc = (re + made[:3], im + made[3:])
        odd_f[0] = jnp.concatenate(acc, axis=0)
        for c in forth + back:
            c.wait_send()

    def link_sends_end():
        for copies in rim:
            for c in copies:
                c.wait_send()

    opening_half()
    (vec[1],) = second_half([src_b], MASS, lambda: local_matrices(0), lambda: border_matrices(0))
    link_sends_end()
    first_half([vec.at[1]], None, lambda: border_matrices(1))
    (vec[2],) = second_half([vec.at[1]], MASS)

    def block(blk, carry):
        diagonal = MASS - shift[...]
        first_half([vec.at[2]], lambda: stage_start(blk, 0, local_dots()))
        (vec[3],) = second_half(
            [vec.at[2]], diagonal, lambda: stage_start(blk, 1, stage_end(blk, 0))
        )
        first_half([vec.at[3]])
        parts = []
        (fourth,) = second_half(
            [vec.at[3]], diagonal, lambda: parts.extend(early_update(stage_end(blk, 1)))
        )
        late_update(parts, fourth)
        return carry

    lax.fori_loop(0, BLOCKS - 2, block, 0)

    blk, last = BLOCKS - 2, BLOCKS - 1
    c = shift[...]
    first_half([vec.at[2]], lambda: stage_start(blk, 0, local_dots()))
    (vec[3],) = second_half(
        [vec.at[2]], MASS - c, lambda: stage_start(blk, 1, stage_end(blk, 0))
    )
    known = []

    def steps_and_iterates():
        line = stage_end(blk, 1)
        a, b, _ = coefficients([spread(line, n) for n in range(DOTS)])
        iterates((a, b), a[2] * vec[0] + a[3] * vec[1] + a[4] * prev[0])
        known.extend((a, b, moments()))

    first_half([vec.at[3]], steps_and_iterates)
    ready = known.pop()
    both = [xs.at[0], xs.at[1]]

    def last_moment():
        odd = odd_f[0]
        stage_start(last, 0, ready + jnp.where(lane == 20, jnp.sum(odd * odd), 0.0))

    (value,), odds = two_halves([odd_f.at[0]], both, last_moment)
    odd_f[1], odd_f[2] = odds
    fourth = (MASS - c) * vec[3] - value
    (_, _, u, f, h), (_, _, u1, f1, h1) = known
    powers = [vec[0], vec[1], vec[2], vec[3], fourth]
    before = [u * powers[k] + f * powers[k + 1] + h * prev[k] for k in range(4)]
    after = [u1 * before[k] + f1 * before[k + 1] + h1 * powers[k] for k in range(3)]
    stage_start(last, 1, stage_end(last, 0))
    values = half([odd_f.at[1], odd_f.at[2]], 0, base=1)
    for n in range(2):
        images[n] = MASS * xs[n] - values[n]
    last_update(dots_from(stage_end(last, 1), known, c), *after, *before[:2])


def per_device(source, fat_links, long_links):
    f32 = jnp.float32
    field = (6, *TILE)
    dma = pltpu.SemaphoreType.DMA
    fat = fat_links.reshape(2, 4, 18, *TILE)
    long = long_links.reshape(2, 4, 18, *TILE)
    vmem = pl.BlockSpec(memory_space=pltpu.VMEM)
    hbm = pl.BlockSpec(memory_space=pltpu.HBM)
    x, t = pl.pallas_call(
        kernel,
        out_shape=(pltpu.VMEM(field, f32), pltpu.VMEM(field, f32)),
        in_specs=[hbm] * 3,
        out_specs=(vmem, vmem),
        scratch_shapes=[
            pltpu.VMEM(fat.shape, fat.dtype),
            pltpu.VMEM(long.shape, long.dtype),
            pltpu.VMEM(field, f32),
            pltpu.VMEM((4, *field), f32),
            pltpu.VMEM((4, *field), f32),
            pltpu.VMEM((2, *field), f32),
            pltpu.VMEM((2, *field), f32),
            pltpu.VMEM((3, *field), f32),
            pltpu.VMEM((2, 16, 18, *TILE), f32),
            pltpu.VMEM((3, 2, *field), f32),
            pltpu.VMEM((2, 3, 3, 2, *field), f32),
            pltpu.VMEM((2, 3, 2, 18, *TILE), jnp.bfloat16),
            pltpu.VMEM((1, 128), f32),
            pltpu.VMEM((2, BLOCKS, MEMBERS, 1, 128), f32),
            pltpu.VMEM(TILE, f32),
            pltpu.VMEM(TILE, f32),
            dma((5,)),
            dma((2, 3, 3, 2)),
            dma((2, 3, 3, 2)),
            dma((2, 3, 2)),
            dma((2, 3, 2)),
            dma((MEMBERS - 1,)),
            dma((2, BLOCKS, MEMBERS)),
        ],
        compiler_params=pltpu.CompilerParams(
            collective_id=0, has_side_effects=True
        ),
    )(source.reshape(field), fat, long)
    return x.reshape(source.shape), t.reshape(source.shape)


def solution(mesh):
    field = P(None, None, "ta", "gz", "gy")
    links = P(None, None, None, None, None, "ta", "gz", "gy")
    return jax.shard_map(
        per_device,
        mesh=mesh,
        in_specs=(field, links, links),
        out_specs=(field, field),
        check_vma=False,
    )
```
